32 devices in a mesh: dp: 8 (over z, y), mp: 4 (over x, core).
Axes of the slice: x: 2, y: 2, z: 4, core: 2. Of those that a mesh axis runs over, the one named last changes fastest.
Arguments:
- tokens: bfloat16 [8192, 1024], P(('dp', 'mp')), may hold values from -6 to 6
- cotangent: bfloat16 [8192, 1024], P(('dp', 'mp')), may hold values from -6 to 6
- segments: int32 [8192], P('dp'), may hold values from 0 to 21, as said below
- lengths: int32 [8, 21], P('dp'), may hold values from 0 to 1024, as said below
- scale_levels: int32 [8], P('dp'), may hold values from 0 to 3
- first_gain: float32 [1024], replicated, may hold values from 0.5 to 1.5
- first_shift: float32 [1024], replicated, may hold values from -3 to 3
- input_weight: bfloat16 [3, 1024, 1024], P(None, None, 'mp'), may hold values from -0.1875 to 0.1875
- input_bias: float32 [2, 1024], P(None, 'mp'), may hold values from -3 to 3
- output_weight: bfloat16 [1024, 1024], P('mp'), may hold values from -0.75 to 0.75
- output_bias: float32 [1024], replicated, may hold values from -3 to 3
- second_gain: float32 [1024], replicated, may hold values from 0.5 to 1.5
- second_shift: float32 [1024], replicated, may hold values from -3 to 3
- expand_weight: bfloat16 [1024, 4096], P(None, 'mp'), may hold values from -0.1875 to 0.1875
- expand_bias: float32 [4096], P('mp'), may hold values from -3 to 3
- reduce_weight: bfloat16 [4096, 1024], P('mp'), may hold values from -0.09375 to 0.09375
- reduce_bias: float32 [1024], replicated, may hold values from -3 to 3
Outputs:
- block_output: bfloat16 [8192, 1024], P(('dp', 'mp'))
- input_gradient: float32 [8192, 1024], P(('dp', 'mp'))
- first_gain_gradient: float32 [1024], replicated
- first_shift_gradient: float32 [1024], replicated
- input_weight_gradient: float32 [3, 1024, 1024], P(None, None, 'mp')
- input_bias_gradient: float32 [2, 1024], P(None, 'mp')
- output_weight_gradient: float32 [1024, 1024], P('mp')
- output_bias_gradient: float32 [1024], replicated
- second_gain_gradient: float32 [1024], replicated
- second_shift_gradient: float32 [1024], replicated
- expand_weight_gradient: float32 [1024, 4096], P(None, 'mp')
- expand_bias_gradient: float32 [4096], P('mp')
- reduce_weight_gradient: float32 [4096, 1024], P('mp')
- reduce_bias_gradient: float32 [1024], replicated
The draws below stay inside these ranges and needn't reach their ends.
Inputs may be any that keep to these rules, and one draw needn't show every extreme that they name: In each group, slot 0 holds one scene, the next slots hold chips of exactly 49 patches, the rest hold 0; a group's lengths sum to more than 975 and to 1024 at most. Items take consecutive rows in slot order from the group's first row, each as many as its length; rows past the sum of the group's lengths carry 21 (padding); segments agree with lengths.
All inputs are finite; a program needn't handle non-finite values.
Results may differ from the reference program's by a relative error of at most 0.017.
Values may be sent and summed in bfloat16 or wider, within the bound.
No kernel may reach another device: no remote copies, remote signals or barrier semaphores. Data moves between devices by JAX's collectives and lax.ppermute only.
A program may use at most 128 MiB of HBM per device.

```python
import jax
import jax.numpy as jnp
from jax import lax

D = 1024
HEADS = 16
HD = 64
FF = 4096
CHIP = 49
NGSD = 4
GROUP = 1024
GROUPS = 8
TOKENS = 8192
ITEMS = 21


def packing(key):
    draw_key = jax.random.fold_in(key, 17)
    group_index = jnp.arange(GROUPS, dtype=jnp.int32)
    scene_drawn = GROUP // 4 + jax.random.randint(draw_key, (GROUPS,), 0, 3 * GROUP // 4 + 1)
    scene_length = jnp.where(group_index == GROUPS - 1, GROUP, scene_drawn).astype(jnp.int32)
    chip_count = (GROUP - scene_length) // CHIP
    slot_index = jnp.arange(ITEMS, dtype=jnp.int32)
    chip_part = jnp.where(slot_index[None, :] <= chip_count[:, None], CHIP, 0)
    return jnp.where(slot_index[None, :] == 0, scene_length[:, None], chip_part).astype(jnp.int32)


def draw_lengths(key, part):
    return packing(key)


def draw_segments(key, part):
    item_lengths = packing(key)
    item_ends = jnp.cumsum(item_lengths, 1).astype(jnp.int32)
    row_index = jnp.arange(GROUP, dtype=jnp.int32)
    item_rows = jnp.sum((item_ends[:, None, :] <= row_index[None, :, None]).astype(jnp.int32), 2)
    return item_rows.reshape(GROUPS * GROUP).astype(jnp.int32)


def plant(array, own_key, least, largest):
    longest = array.shape.index(max(array.shape))
    spots = []
    for shift in (0, 1):
        where = [jax.random.randint(jax.random.fold_in(own_key, axis), (), 0, length) for axis, length in enumerate(array.shape)]
        where[longest] = (where[longest] + shift) % array.shape[longest]
        spots.append(tuple(where))
    return array.at[spots[0]].set(least).at[spots[1]].set(largest)


def levels(rng, extent, cuts, least, high):
    def one(axis_at, blocks):
        heights = jax.random.uniform(jax.random.fold_in(jax.random.fold_in(rng, 6), axis_at), (blocks,), jnp.float32, least / len(cuts), high / len(cuts))
        return jnp.repeat(jnp.exp(heights), extent[axis_at] // blocks).reshape((-1,) + (1,) * (len(extent) - axis_at - 1))

    factor_of = one(*cuts[0])
    for cut in cuts[1:]:
        factor_of = factor_of * one(*cut)
    return factor_of


def centred(rng, shape, width, most, pieces=(), held_as=jnp.bfloat16):
    result = width * jax.random.normal(rng, shape, jnp.float32)
    if pieces:
        result = result * levels(rng, shape, pieces, -0.22, 0.18)
    return jnp.clip(result, -most, most).astype(held_as)


def setup_inputs(seed: int = 0) -> dict:
    keys = jax.random.split(jax.random.key(seed), 18)
    return {
        "tokens": centred(keys[0], (TOKENS, D), 1.0, 6.0, ((0, 32),)),
        "cotangent": centred(keys[1], (TOKENS, D), 1.0, 6.0, ((0, 32),)),
        "segments": draw_segments(jax.random.fold_in(keys[17], 71), 0),
        "lengths": draw_lengths(jax.random.fold_in(keys[17], 71), 0),
        "scale_levels": plant(jax.random.randint(keys[4], (GROUPS,), 0, NGSD), jax.random.fold_in(keys[4], 1), 0, NGSD - 1).astype(jnp.int32),
        "first_gain": jnp.clip(1.0 + 0.1 * jax.random.normal(keys[5], (D,), jnp.float32), 0.5, 1.5),
        "first_shift": centred(keys[6], (D,), 0.5, 3.0, (), jnp.float32),
        "input_weight": centred(keys[7], (3, D, D), D ** -0.5, 0.1875, ((2, 4),)),
        "input_bias": centred(keys[8], (2, D), 0.5, 3.0, ((1, 4),), jnp.float32),
        "output_weight": centred(keys[9], (D, D), (D // 16) ** -0.5, 0.75, ((0, 4),)),
        "output_bias": centred(keys[10], (D,), 0.5, 3.0, (), jnp.float32),
        "second_gain": jnp.clip(1.0 + 0.1 * jax.random.normal(keys[11], (D,), jnp.float32), 0.5, 1.5),
        "second_shift": centred(keys[12], (D,), 0.5, 3.0, (), jnp.float32),
        "expand_weight": centred(keys[13], (D, FF), D ** -0.5, 0.1875, ((1, 4),)),
        "expand_bias": centred(keys[14], (FF,), 0.5, 3.0, ((0, 4),), jnp.float32),
        "reduce_weight": centred(keys[15], (FF, D), FF ** -0.5, 0.09375, ((0, 4),)),
        "reduce_bias": centred(keys[16], (D,), 0.5, 3.0, (), jnp.float32),
    }


@jax.custom_vjp
def low(v):
    return lax.optimization_barrier(v.astype(jnp.bfloat16)).astype(jnp.float32)

@jax.custom_vjp
def low_back(v):
    return v

def low_keep(v):
    return (low(v), None)

def low_pass(kept, grad):
    return (grad,)

def back_keep(v):
    return (v, None)

def back_low(kept, grad):
    return (low(grad),)
low.defvjp(low_keep, low_pass)
low_back.defvjp(back_keep, back_low)

def matmul_high(left_side, right_side):
    return jnp.dot(left_side, right_side, precision=lax.Precision.HIGHEST)

def normalize(values, gain, shift):
    center = values - lax.optimization_barrier(jnp.mean(values, -1, keepdims=True))
    inverse = lax.rsqrt(lax.optimization_barrier(jnp.mean(center * center, -1, keepdims=True)) + 1e-06)
    return center * inverse * gain + shift

def position_rows(item_rows, item_lengths, level):
    item_ends = jnp.cumsum(item_lengths).astype(jnp.int32)
    starts = item_ends - item_lengths
    slot_index = jnp.arange(ITEMS, dtype=jnp.int32)
    start_row = lax.optimization_barrier(jnp.sum(jnp.where(item_rows[:, None] == slot_index[None, :], starts[None, :], 0), 1))
    row_index = jnp.arange(GROUP, dtype=jnp.int32)
    valid_rows = (item_rows < ITEMS).astype(jnp.float32)
    level_ratio = jnp.exp2(level.astype(jnp.float32) - 2.0)
    places = (row_index - start_row).astype(jnp.float32) * level_ratio
    half_width = D // 2
    frequency = jnp.exp(-jnp.log(10000.0) * jnp.arange(half_width, dtype=jnp.float32) / half_width)
    angles = places[:, None] * frequency[None, :]
    return (jnp.concatenate([jnp.sin(angles), jnp.cos(angles)], 1) * valid_rows[:, None], valid_rows)

def attention(query_rows, key_rows, value_rows, item_rows):
    block_rows = min(512, GROUP)
    score_scale = HD ** (-0.5)
    keys_view = key_rows.reshape(GROUP, HEADS, HD)
    values_view = value_rows.reshape(GROUP, HEADS, HD)
    query_blocks = query_rows.reshape(GROUP // block_rows, block_rows, HEADS, HD)
    item_blocks = item_rows.reshape(GROUP // block_rows, block_rows)

    def attend_block(inputs):
        query_block, item_block = inputs
        scores = jnp.einsum('bhe,khe->hbk', query_block, keys_view, precision=lax.Precision.HIGHEST) * score_scale
        scores = low_back(scores)
        same_item = item_block[None, :, None] == item_rows[None, None, :]
        scores = jnp.where(same_item, scores, -1e+30)
        row_max = lax.optimization_barrier(jnp.max(scores, -1, keepdims=True))
        exp_scores = jnp.exp(scores - row_max)
        weights = exp_scores / lax.optimization_barrier(jnp.sum(exp_scores, -1, keepdims=True))
        return jnp.einsum('hbk,khe->bhe', low(weights), values_view, precision=lax.Precision.HIGHEST)
    attended = lax.map(jax.checkpoint(attend_block), (query_blocks, item_blocks))
    return attended.reshape(GROUP, HEADS * HD)

def forward(params, tokens_in, item_rows, positions):
    first_gain, first_shift, input_weight, input_bias, output_weight, output_bias, second_gain, second_shift, expand_weight, expand_bias, reduce_weight, reduce_bias = params
    residual = tokens_in + positions
    attn_input = low(normalize(residual, first_gain, first_shift))
    query_rows = low(low_back(matmul_high(attn_input, input_weight[0]) + input_bias[0]))
    key_rows = low(low_back(matmul_high(attn_input, input_weight[1])))
    value_rows = low(low_back(matmul_high(attn_input, input_weight[2]) + input_bias[1]))
    heads_out = low(low_back(attention(query_rows, key_rows, value_rows, item_rows)))
    hidden_rows = residual + low_back(matmul_high(heads_out, output_weight) + output_bias)
    mlp_input = low(normalize(hidden_rows, second_gain, second_shift))
    pre_act = low_back(matmul_high(mlp_input, expand_weight) + expand_bias)
    activated = low(jax.nn.gelu(pre_act, approximate=False))
    return hidden_rows + low_back(matmul_high(activated, reduce_weight) + reduce_bias)

def reference(tokens, cotangent, segments, lengths, scale_levels, first_gain, first_shift, input_weight, input_bias, output_weight, output_bias, second_gain, second_shift, expand_weight, expand_bias, reduce_weight, reduce_bias):
    params = tuple((weight.astype(jnp.float32) for weight in (first_gain, first_shift, input_weight, input_bias, output_weight, output_bias, second_gain, second_shift, expand_weight, expand_bias, reduce_weight, reduce_bias)))
    token_groups = tokens.astype(jnp.float32).reshape(GROUPS, GROUP, D)
    cotangent_groups = cotangent.astype(jnp.float32).reshape(GROUPS, GROUP, D)
    item_groups = segments.reshape(GROUPS, GROUP)

    def per_group(running, group_data):
        tokens_in, cotangent_in, item_rows, item_lengths, level = group_data
        positions, valid_rows = position_rows(item_rows, item_lengths, level)
        outputs, pullback = jax.vjp(lambda weights, values: forward(weights, values, item_rows, positions), params, tokens_in)
        param_grads, token_grads = pullback(cotangent_in * valid_rows[:, None])
        running = tuple((total + extra for total, extra in zip(running, param_grads)))
        return (running, (outputs.astype(jnp.bfloat16), token_grads))
    zero_grads = tuple((jnp.zeros_like(weight) for weight in params))
    running, (outputs, token_grads) = lax.scan(per_group, zero_grads, (token_groups, cotangent_groups, item_groups, lengths, scale_levels))
    factor = lax.rsqrt(jnp.sum(lengths).astype(jnp.float32))
    return (outputs.reshape(TOKENS, D), token_grads.reshape(TOKENS, D), running[0] * factor, running[1] * factor, running[2] * factor, running[3] * factor, running[4] * factor, running[5] * factor, running[6] * factor, running[7] * factor, running[8] * factor, running[9] * factor, running[10] * factor, running[11] * factor)
```

```python
import jax
import jax.numpy as jnp
from jax import lax
from jax.sharding import PartitionSpec as P

HD = 64
EPSILON = 1e-06
EXCLUDED = -1e30
F32 = jnp.float32
BF16 = jnp.bfloat16


def row_contract(left_side, right_side):
    return lax.dot_general(
        left_side, right_side, (((0,), (0,)), ((), ())), preferred_element_type=F32
    )


def column_contract(left_side, right_side):
    return lax.dot_general(
        left_side, right_side, (((1,), (1,)), ((), ())), preferred_element_type=F32
    )


def normalize(values):
    center = values - jnp.mean(values, -1, keepdims=True)
    inverse = lax.rsqrt(jnp.mean(center * center, -1, keepdims=True) + EPSILON)
    return (center * inverse, inverse)


def normalize_back(upstream, normed, inverse, gain):
    scaled = upstream * gain
    return inverse * (
        scaled
        - jnp.mean(scaled, -1, keepdims=True)
        - normed * jnp.mean(scaled * normed, -1, keepdims=True)
    )


def position_rows(own_items, item_lengths, level, first_row, width):
    slot_count = item_lengths.shape[0]
    item_ends = jnp.cumsum(item_lengths)
    starts = item_ends - item_lengths
    slot_index = lax.broadcasted_iota(jnp.int32, (1, slot_count), 1)
    start_row = jnp.sum(jnp.where(own_items[:, None] == slot_index, starts[None, :], 0), 1)
    row_index = first_row + jnp.arange(own_items.shape[0], dtype=jnp.int32)
    valid_rows = (own_items < slot_count).astype(F32)
    level_ratio = jnp.exp2(level.astype(F32) - 2.0)
    places = (row_index - start_row).astype(F32) * level_ratio
    half_width = width // 2
    frequency = jnp.exp(-jnp.log(10000.0) * jnp.arange(half_width, dtype=F32) / half_width)
    angles = places[:, None] * frequency[None, :]
    return (
        jnp.concatenate([jnp.sin(angles), jnp.cos(angles)], 1) * valid_rows[:, None],
        valid_rows,
    )


def bits_of(size):
    bits = []
    step = 1
    while step < size:
        bits.append(step)
        step *= 2
    return bits


def swap(array, axis, size, bit):
    return lax.ppermute(array, axis, [(i, i ^ bit) for i in range(size)])


def gather_rows(own, count):
    blocks = {0: own}
    for bit in reversed(bits_of(count)):
        blocks.update(
            {j | bit: swap(rows, "mp", count, bit) for j, rows in list(blocks.items())}
        )
    return [blocks[j] for j in range(count)]


def scatter_rows(blocks, count):
    held = {j: block for j, block in enumerate(blocks)}
    for bit in bits_of(count):
        arrived = {
            j ^ bit: swap(held[j].astype(BF16), "mp", count, bit)
            for j in held
            if j & bit
        }
        held = {j: held[j].astype(F32) + arrived[j].astype(F32) for j in arrived}
    return held[0]


def row_blocks(array, count):
    size = array.shape[0] // count
    return [array[j * size : (j + 1) * size] for j in range(count)]


def dp_sum(parts, count, index, axis):
    held = parts
    for bit in bits_of(count):
        half = held.shape[axis] // 2
        high = jnp.where((index & bit) != 0, 1, 0)
        keep = lax.dynamic_slice_in_dim(held, high * half, half, axis)
        send = lax.dynamic_slice_in_dim(held, (1 - high) * half, half, axis)
        held = keep.astype(F32) + swap(send.astype(BF16), "dp", count, bit).astype(F32)
    held = held.astype(BF16)
    for bit in reversed(bits_of(count)):
        other = swap(held, "dp", count, bit)
        high = (index & bit) != 0
        held = jnp.where(
            high, jnp.concatenate([other, held], axis), jnp.concatenate([held, other], axis)
        )
    return held


def butterfly(values, sizes):
    for axis, size in sizes:
        for bit in bits_of(size):
            values = values + swap(values, axis, size, bit)
    return values


def attend_forward(query_rows, key_rows, value_rows, segments):
    score_scale = query_rows.shape[2] ** (-0.5)
    scores = (
        jnp.einsum("bhe,khe->hbk", query_rows, key_rows, preferred_element_type=F32) * score_scale
    )
    same_item = segments[None, :, None] == segments[None, None, :]
    scores = jnp.where(same_item, scores, EXCLUDED)
    row_max = jnp.max(scores, -1, keepdims=True)
    exp_scores = jnp.exp(scores - row_max)
    row_total = jnp.sum(exp_scores, -1, keepdims=True)
    prob_low = (exp_scores / row_total).astype(BF16)
    attended = jnp.einsum("hbk,khe->bhe", prob_low, value_rows, preferred_element_type=F32)
    return (attended, row_max[..., 0] + jnp.log(row_total[..., 0]))


def attend_back(query_rows, key_rows, value_rows, head_grads, log_totals, segments):
    score_scale = query_rows.shape[2] ** (-0.5)
    scores = (
        jnp.einsum("bhe,khe->hbk", query_rows, key_rows, preferred_element_type=F32) * score_scale
    )
    same_item = segments[None, :, None] == segments[None, None, :]
    prob_full = jnp.where(same_item, jnp.exp(scores - log_totals[:, :, None]), 0.0)
    prob_low = prob_full.astype(BF16)
    value_sum = jnp.einsum("hbk,bhe->khe", prob_low, head_grads, preferred_element_type=F32)
    prob_grad = jnp.einsum("bhe,khe->hbk", head_grads, value_rows, preferred_element_type=F32)
    center = jnp.sum(prob_grad * prob_full, -1, keepdims=True)
    score_grad = (prob_full * (prob_grad - center)).astype(BF16)
    query_grad = (
        jnp.einsum("hbk,khe->bhe", score_grad, key_rows, preferred_element_type=F32) * score_scale
    )
    key_sum = (
        jnp.einsum("hbk,bhe->khe", score_grad, query_rows, preferred_element_type=F32) * score_scale
    )
    return (query_grad, key_sum, value_sum)


def layer(sizes):
    n_dp, n_mp = sizes

    def per_device(
        tokens,
        cotangent,
        segments,
        lengths,
        scale_levels,
        first_gain,
        first_shift,
        input_weight,
        input_bias,
        output_weight,
        output_bias,
        second_gain,
        second_shift,
        expand_weight,
        expand_bias,
        reduce_weight,
        reduce_bias,
    ):
        me = lax.axis_index("mp")
        group = lax.axis_index("dp")
        own_count, width = tokens.shape
        local_width = input_weight.shape[2]
        head_count = local_width // HD
        item_blocks = [
            lax.dynamic_slice_in_dim(segments, (me ^ j) * own_count, own_count)
            for j in range(n_mp)
        ]
        items = jnp.concatenate(item_blocks)
        positions, valid_rows = position_rows(
            item_blocks[0], lengths[0], scale_levels[0], me * own_count, width
        )
        group_patches = jnp.sum(lengths).astype(F32)
        residual = tokens.astype(F32) + positions
        normed_one, inverse_one = normalize(residual)
        attn_input = (normed_one * first_gain + first_shift).astype(BF16)
        attn_rows = jnp.concatenate(gather_rows(attn_input, n_mp))
        grad_out = cotangent.astype(F32) * valid_rows[:, None]
        grad_all = jnp.concatenate(gather_rows(grad_out.astype(BF16), n_mp))
        reduce_bias_part = jnp.sum(grad_out, 0)

        projected = jnp.einsum("rd,tde->tre", attn_rows, input_weight, preferred_element_type=F32)
        bias_rows = jnp.stack([input_bias[0], jnp.zeros_like(input_bias[0]), input_bias[1]])
        group_rows = n_mp * own_count
        qkv_rows = (
            (projected + bias_rows[:, None, :])
            .astype(BF16)
            .reshape(3, group_rows, head_count, HD)
        )
        query_rows, key_rows, value_rows = (qkv_rows[0], qkv_rows[1], qkv_rows[2])
        attended, log_totals = attend_forward(query_rows, key_rows, value_rows, items)
        heads_out = attended.astype(BF16).reshape(group_rows, local_width)
        attn_sum = scatter_rows(
            row_blocks(jnp.dot(heads_out, output_weight, preferred_element_type=F32), n_mp), n_mp
        )
        hidden_res = residual + attn_sum + output_bias
        normed_two, inverse_two = normalize(hidden_res)
        mlp_input = (normed_two * second_gain + second_shift).astype(BF16)
        mlp_rows = jnp.concatenate(gather_rows(mlp_input, n_mp))
        pre_act = jnp.dot(mlp_rows, expand_weight, preferred_element_type=F32) + expand_bias
        cdf = 0.5 * (1.0 + lax.erf(pre_act * (0.5**0.5)))
        activated = (pre_act * cdf).astype(BF16)
        act_grad = column_contract(grad_all, reduce_weight)
        slope = cdf + pre_act * jnp.exp(-0.5 * pre_act * pre_act) * 0.3989422804014327
        pre_grad = (act_grad * slope).astype(BF16)
        activated, pre_grad = lax.optimization_barrier((activated, pre_grad))
        normed_grad_two = scatter_rows(
            row_blocks(column_contract(pre_grad, expand_weight), n_mp), n_mp
        )
        reduce_grad = dp_sum(row_contract(activated, grad_all), n_dp, group, 0)
        expand_grad = dp_sum(row_contract(mlp_rows, pre_grad), n_dp, group, 0)
        expand_bias_grad = jnp.sum(pre_grad, 0, dtype=F32)
        mlp_sum = scatter_rows(
            row_blocks(jnp.dot(activated, reduce_weight, preferred_element_type=F32), n_mp), n_mp
        )
        block_output = (hidden_res + mlp_sum + reduce_bias).astype(BF16)
        gain_two_part = jnp.sum(normed_grad_two * normed_two, 0)
        shift_two_part = jnp.sum(normed_grad_two, 0)
        residual_grad = grad_out + normalize_back(
            normed_grad_two, normed_two, inverse_two, second_gain
        )
        branch_grad = residual_grad.astype(BF16)
        out_bias_part = jnp.sum(branch_grad, 0, dtype=F32)
        branch_all = jnp.concatenate(gather_rows(branch_grad, n_mp))
        output_grad = dp_sum(row_contract(heads_out, branch_all), n_dp, group, 0)
        head_grads = column_contract(branch_all, output_weight).astype(BF16)
        query_grad, key_grad, value_grad = attend_back(
            query_rows,
            key_rows,
            value_rows,
            head_grads.reshape(group_rows, head_count, HD),
            log_totals,
            items,
        )
        qkv_grad = (
            jnp.stack([query_grad, key_grad, value_grad])
            .astype(BF16)
            .reshape(3, group_rows, local_width)
        )
        qv_grad = jnp.stack(
            [jnp.sum(qkv_grad[0], 0, dtype=F32), jnp.sum(qkv_grad[2], 0, dtype=F32)]
        )
        input_grad = dp_sum(
            jnp.einsum("rd,tre->tde", attn_rows, qkv_grad, preferred_element_type=F32),
            n_dp,
            group,
            1,
        )
        normed_grad_one = scatter_rows(
            row_blocks(
                jnp.einsum("tre,tde->rd", qkv_grad, input_weight, preferred_element_type=F32), n_mp
            ),
            n_mp,
        )
        gain_one_part = jnp.sum(normed_grad_one * normed_one, 0)
        shift_one_part = jnp.sum(normed_grad_one, 0)
        input_gradient = residual_grad + normalize_back(
            normed_grad_one, normed_one, inverse_one, first_gain
        )
        both = (("dp", n_dp), ("mp", n_mp))
        early = butterfly(
            jnp.stack([gain_two_part, shift_two_part, out_bias_part, reduce_bias_part]), both
        )
        local = butterfly(
            jnp.concatenate([expand_bias_grad, jnp.full((128,), group_patches)])[None],
            (("dp", n_dp),),
        )[0]
        expand_bias_total = local[: expand_bias_grad.shape[0]]
        factor = lax.rsqrt(local[expand_bias_grad.shape[0]])
        late = butterfly(jnp.stack([gain_one_part, shift_one_part]), both)
        qv_total = butterfly(qv_grad, (("dp", n_dp),))
        return (
            block_output,
            input_gradient,
            late[0] * factor,
            late[1] * factor,
            input_grad.astype(F32) * factor,
            qv_total * factor,
            output_grad.astype(F32) * factor,
            early[2] * factor,
            early[0] * factor,
            early[1] * factor,
            expand_grad.astype(F32) * factor,
            expand_bias_total * factor,
            reduce_grad.astype(F32) * factor,
            early[3] * factor,
        )

    return per_device


def solution(mesh):
    placed = (
        P(("dp", "mp"), None),
        P(("dp", "mp"), None),
        P("dp"),
        P("dp", None),
        P("dp"),
        P(),
        P(),
        P(None, None, "mp"),
        P(None, "mp"),
        P("mp", None),
        P(),
        P(),
        P(),
        P(None, "mp"),
        P("mp"),
        P("mp", None),
        P(),
    )
    return jax.shard_map(
        layer((mesh.shape["dp"], mesh.shape["mp"])),
        mesh=mesh,
        in_specs=placed,
        out_specs=(
            P(("dp", "mp"), None),
            P(("dp", "mp"), None),
            P(),
            P(),
            P(None, None, "mp"),
            P(None, "mp"),
            P("mp", None),
            P(),
            P(),
            P(),
            P(None, "mp"),
            P("mp"),
            P("mp", None),
            P(),
        ),
        check_vma=False,
    )
```

```python
import functools
import jax
import jax.numpy as jnp
from jax import lax
from jax.experimental import pallas as pl
from jax.experimental.pallas import tpu as pltpu
from jax.sharding import PartitionSpec as P

F32 = jnp.float32
BF16 = jnp.bfloat16
PAIR = 128
HD = 64
EXCLUDED = -1e30


def dot_nn(a, b):
    return lax.dot_general(a, b, (((1,), (0,)), ((), ())), preferred_element_type=F32)


def dot_nt(a, b):
    return lax.dot_general(a, b, (((1,), (1,)), ((), ())), preferred_element_type=F32)


def dot_tn(a, b):
    return lax.dot_general(a, b, (((0,), (0,)), ((), ())), preferred_element_type=F32)


def head_lanes(head):
    lane = lax.broadcasted_iota(jnp.int32, (1, PAIR), 1)
    return (lane >= head * HD) & (lane < (head + 1) * HD)


def attend_kernel(halves, q_ref, pick_ref, *refs):
    k_refs, v_refs, bar_refs = (
        refs[:halves],
        refs[halves : 2 * halves],
        refs[2 * halves : 3 * halves],
    )
    out_ref, log_ref = refs[3 * halves :]
    query = q_ref[0]
    scaled = query * jnp.asarray(HD**-0.5, BF16)
    pick = pick_ref[...]
    keys = [jnp.concatenate([k[0], b[...]], 1) for k, b in zip(k_refs, bar_refs)]
    rows = []
    for head in range(2):
        own = jnp.where(head_lanes(head), scaled, jnp.zeros_like(scaled))
        probe = jnp.concatenate([own, pick], 1)
        scores = [dot_nt(k, probe) for k in keys]
        top = functools.reduce(
            jnp.maximum, [jnp.max(s, 0, keepdims=True) for s in scores]
        )
        powers = [jnp.exp(s - top) for s in scores]
        total = functools.reduce(
            jnp.add, [jnp.sum(p, 0, keepdims=True) for p in powers]
        )
        summed = functools.reduce(
            jnp.add, [dot_tn(v[0], p.astype(BF16)) for v, p in zip(v_refs, powers)]
        )
        rows.append((summed / total)[head * HD : (head + 1) * HD])
        log_ref[0, head : head + 1, :] = top + jnp.log(total)
    out_ref[...] = jnp.concatenate(rows, 0).T.astype(BF16)


def attend_forward(query, pick, keys, values, bars, tile=256):
    _, count, width = query.shape
    halves = len(keys)
    pairs = width // PAIR
    tile = min(tile, count)
    grid = (pairs, count // tile)
    key_spec = [pl.BlockSpec((1, k.shape[1], PAIR), lambda p, i: (0, 0, p)) for k in keys]
    bar_spec = [pl.BlockSpec((b.shape[0], PAIR), lambda p, i: (0, 0)) for b in bars]
    total_keys = sum(k.shape[1] for k in keys)
    return pl.pallas_call(
        functools.partial(attend_kernel, halves),
        grid=grid,
        in_specs=[
            pl.BlockSpec((1, tile, PAIR), lambda p, i: (0, i, p)),
            pl.BlockSpec((tile, PAIR), lambda p, i: (i, 0)),
            *key_spec,
            *key_spec,
            *bar_spec,
        ],
        out_specs=[
            pl.BlockSpec((tile, PAIR), lambda p, i: (i, p)),
            pl.BlockSpec((1, 8, tile), lambda p, i: (p, 0, i)),
        ],
        out_shape=[
            jax.ShapeDtypeStruct((count, width), BF16),
            jax.ShapeDtypeStruct((pairs, 8, count), F32),
        ],
        cost_estimate=pl.CostEstimate(
            flops=16 * count * total_keys * width,
            bytes_accessed=6 * total_keys * width,
            transcendentals=count * total_keys * width // HD,
        ),
        name="attend_forward",
    )(query, pick, *keys, *values, *bars)


def attend_back_kernel(halves, first, last, q_ref, pick_ref, grad_ref, out_ref, log_ref, *refs):
    k_refs, v_refs, bar_refs = (
        refs[:halves],
        refs[halves : 2 * halves],
        refs[2 * halves : 3 * halves],
    )
    rest = refs[3 * halves :]
    if not first:
        k_in, v_in = rest[:halves], rest[halves : 2 * halves]
        rest = rest[2 * halves :]
    q_grad_ref = rest[0]
    k_out, v_out = rest[1 : 1 + halves], rest[1 + halves : 1 + 2 * halves]
    if last:
        k_sum, v_sum = (
            rest[1 + 2 * halves : 1 + 3 * halves],
            rest[1 + 3 * halves : 1 + 4 * halves],
        )
    else:
        k_sum, v_sum = k_out, v_out
    step = pl.program_id(1)

    @pl.when(step == 0)
    def _():
        for n in range(halves):
            if first:
                k_sum[n][...] = jnp.zeros_like(k_sum[n])
                v_sum[n][...] = jnp.zeros_like(v_sum[n])
            else:
                k_sum[n][...] = k_in[n][...]
                v_sum[n][...] = v_in[n][...]

    scaled = q_ref[0] * jnp.asarray(HD**-0.5, BF16)
    grad = grad_ref[...]
    pick = pick_ref[...]
    both = (grad.astype(F32) * out_ref[...].astype(F32)).T
    owns = [jnp.where(head_lanes(h), scaled, jnp.zeros_like(scaled)) for h in range(2)]
    grads = [jnp.where(head_lanes(h), grad, jnp.zeros_like(grad)) for h in range(2)]
    probes = [jnp.concatenate([own, pick], 1) for own in owns]
    centers = [jnp.sum(both[h * HD : (h + 1) * HD], 0, keepdims=True) for h in range(2)]
    stacked_q = jnp.concatenate(owns, 0)
    stacked_g = jnp.concatenate(grads, 0)
    q_parts = [0.0, 0.0]
    for n in range(halves):
        keys = k_refs[n][0]
        values = v_refs[n][0]
        wide = jnp.concatenate([keys, bar_refs[n][...]], 1)
        probs = []
        slopes = []
        for h in range(2):
            prob = jnp.exp(dot_nt(wide, probes[h]) - log_ref[0, h : h + 1, :])
            slope = (prob * (dot_nt(values, grads[h]) - centers[h])).astype(BF16)
            probs.append(prob.astype(BF16))
            slopes.append(slope)
            q_parts[h] = q_parts[h] + dot_tn(keys, slope)
        v_sum[n][...] += dot_nn(jnp.concatenate(probs, 1), stacked_g)
        k_sum[n][...] += dot_nn(jnp.concatenate(slopes, 1), stacked_q)
    rows = [q_parts[h][h * HD : (h + 1) * HD] * (HD**-0.5) for h in range(2)]
    q_grad_ref[...] = jnp.concatenate(rows, 0).T.astype(BF16)

    if last:

        @pl.when(step == pl.num_programs(1) - 1)
        def _():
            for n in range(halves):
                k_out[n][...] = k_sum[n][...].astype(BF16)
                v_out[n][...] = v_sum[n][...].astype(BF16)


def attend_back(query, pick, grad, out, logs, keys, values, bars, carried, last, tile=256):
    _, count, width = query.shape
    halves = len(keys)
    pairs = width // PAIR
    tile = min(tile, count)
    first = carried is None
    key_spec = [pl.BlockSpec((1, k.shape[1], PAIR), lambda p, i: (0, 0, p)) for k in keys]
    bar_spec = [pl.BlockSpec((b.shape[0], PAIR), lambda p, i: (0, 0)) for b in bars]
    sum_spec = [pl.BlockSpec((k.shape[1], PAIR), lambda p, i: (0, p)) for k in keys]
    row_spec = pl.BlockSpec((tile, PAIR), lambda p, i: (i, p))
    sum_type = BF16 if last else F32
    sums = [jax.ShapeDtypeStruct((k.shape[1], width), sum_type) for k in keys]
    total_keys = sum(k.shape[1] for k in keys)
    scratch = []
    if last:
        scratch = [pltpu.VMEM((k.shape[1], PAIR), F32) for k in keys] * 2
    extra = [] if first else list(carried[0]) + list(carried[1])
    result = pl.pallas_call(
        functools.partial(attend_back_kernel, halves, first, last),
        grid=(pairs, count // tile),
        in_specs=[
            pl.BlockSpec((1, tile, PAIR), lambda p, i: (0, i, p)),
            pl.BlockSpec((tile, PAIR), lambda p, i: (i, 0)),
            row_spec,
            row_spec,
            pl.BlockSpec((1, 8, tile), lambda p, i: (p, 0, i)),
            *key_spec,
            *key_spec,
            *bar_spec,
            *([] if first else sum_spec * 2),
        ],
        out_specs=[row_spec, *sum_spec, *sum_spec],
        out_shape=[jax.ShapeDtypeStruct((count, width), BF16), *sums, *sums],
        scratch_shapes=scratch,
        cost_estimate=pl.CostEstimate(
            flops=40 * count * total_keys * width,
            bytes_accessed=16 * total_keys * width,
            transcendentals=count * total_keys * width // HD,
        ),
        name="attend_back",
    )(query, pick, grad, out, logs, *keys, *values, *bars, *extra)
    return result[0], result[1 : 1 + halves], result[1 + halves :]


def mlp_kernel(x_ref, grad_ref, up_ref, bias_ref, down_ref, act_ref, slope_ref, back_ref):
    pre = dot_nn(x_ref[...], up_ref[...]) + bias_ref[...]
    upstream = dot_nt(grad_ref[...], down_ref[...])
    cdf = 0.5 + 0.5 * lax.erf(pre * (0.5**0.5))
    act_ref[...] = (pre * cdf).astype(BF16)
    density = jnp.exp(-0.5 * pre * pre) * 0.3989422804014327
    slope = (upstream * (cdf + pre * density)).astype(BF16)
    slope_ref[...] = slope
    back_ref[...] = dot_nt(slope, up_ref[...]).astype(BF16)


def mlp_both(x, grad, up, bias, down, tile=256):
    count, width = x.shape
    hidden = up.shape[1]
    tile = min(tile, count)
    whole = lambda i: (0, 0)
    return pl.pallas_call(
        mlp_kernel,
        grid=(count // tile,),
        in_specs=[
            pl.BlockSpec((tile, width), lambda i: (i, 0)),
            pl.BlockSpec((tile, width), lambda i: (i, 0)),
            pl.BlockSpec((width, hidden), whole, pipeline_mode=pl.Buffered(1)),
            pl.BlockSpec((1, hidden), whole),
            pl.BlockSpec((hidden, width), whole, pipeline_mode=pl.Buffered(1)),
        ],
        out_specs=[
            pl.BlockSpec((tile, hidden), lambda i: (i, 0)),
            pl.BlockSpec((tile, hidden), lambda i: (i, 0)),
            pl.BlockSpec((tile, width), lambda i: (i, 0)),
        ],
        out_shape=[
            jax.ShapeDtypeStruct((count, hidden), BF16),
            jax.ShapeDtypeStruct((count, hidden), BF16),
            jax.ShapeDtypeStruct((count, width), BF16),
        ],
        cost_estimate=pl.CostEstimate(
            flops=6 * count * width * hidden,
            bytes_accessed=4 * width * hidden + 10 * count * width,
            transcendentals=2 * count * hidden,
        ),
        name="mlp_both",
    )(x, grad, up, bias[None], down)


EPSILON = 1e-06


def normalize(values):
    center = values - jnp.mean(values, -1, keepdims=True)
    inverse = lax.rsqrt(jnp.mean(center * center, -1, keepdims=True) + EPSILON)
    return (center * inverse, inverse)


def normalize_back(upstream, normed, inverse, gain):
    scaled = upstream * gain
    return inverse * (
        scaled
        - jnp.mean(scaled, -1, keepdims=True)
        - normed * jnp.mean(scaled * normed, -1, keepdims=True)
    )


def position_rows(own_items, item_lengths, level, first_row, width):
    slot_count = item_lengths.shape[0]
    slot_index = lax.broadcasted_iota(jnp.int32, (1, slot_count), 1)
    start_row = jnp.sum(jnp.where(slot_index < own_items[:, None], item_lengths[None, :], 0), 1)
    row_index = first_row + jnp.arange(own_items.shape[0], dtype=jnp.int32)
    valid_rows = (own_items < slot_count).astype(F32)
    level_ratio = jnp.exp2(level.astype(F32) - 2.0)
    places = (row_index - start_row).astype(F32) * level_ratio
    half_width = width // 2
    frequency = jnp.exp(-jnp.log(10000.0) * jnp.arange(half_width, dtype=F32) / half_width)
    angles = places[:, None] * frequency[None, :]
    return (
        jnp.concatenate([jnp.sin(angles), jnp.cos(angles)], 1) * valid_rows[:, None],
        valid_rows,
    )


def bits_of(size):
    bits = []
    step = 1
    while step < size:
        bits.append(step)
        step *= 2
    return bits


def tie(*arrays):
    return lax.optimization_barrier(arrays)


def swap(array, axis, size, bit):
    return lax.ppermute(array, axis, [(i, i ^ bit) for i in range(size)])


def gather_near(own, count):
    blocks = {0: own}
    for bit in reversed(bits_of(count)[:-1]):
        blocks.update(
            {j | bit: swap(rows, "mp", count, bit) for j, rows in list(blocks.items())}
        )
    return jnp.concatenate([blocks[j] for j in range(count // 2)])


def scatter_near(rows, count):
    size = rows.shape[0] // (count // 2)
    held = {j: rows[j * size : (j + 1) * size] for j in range(count // 2)}
    for bit in bits_of(count)[:-1]:
        arrived = {
            j ^ bit: swap(held[j].astype(BF16), "mp", count, bit) for j in held if j & bit
        }
        held = {j: held[j].astype(F32) + arrived[j].astype(F32) for j in arrived}
    return held[0]


class DpSum:
    def __init__(self, count, index, order):
        self.count, self.index, self.order = count, index, order

    def high(self, bit):
        return (self.index & bit) != 0

    def open(self, left, right):
        half = left.shape[1] // 2
        top = jnp.where(self.high(self.order[0]), half, 0)
        send = dot_tn(lax.dynamic_slice_in_dim(left, half - top, half, 1), right).astype(BF16)
        self.held = dot_tn(lax.dynamic_slice_in_dim(left, top, half, 1), right).astype(BF16)
        return send

    def split(self, bit):
        half = self.held.shape[0] // 2
        top = jnp.where(self.high(bit), half, 0)
        send = lax.dynamic_slice_in_dim(self.held, half - top, half, 0)
        self.held = lax.dynamic_slice_in_dim(self.held, top, half, 0)
        return send

    def add(self, arrived):
        self.held = (self.held.astype(F32) + arrived.astype(F32)).astype(BF16)

    def join(self, bit, arrived):
        self.held = jnp.where(
            self.high(bit),
            jnp.concatenate([arrived, self.held]),
            jnp.concatenate([self.held, arrived]),
        )

    def pass_on(self, array, bit):
        return swap(array, "dp", self.count, bit)

    def halve_rest(self):
        for bit in self.order[1:]:
            self.add(self.pass_on(self.split(bit), bit))

    def double_all(self):
        for bit in reversed(self.order):
            self.join(bit, self.pass_on(self.held, bit))
        return self.held


def butterfly(values, sizes):
    for axis, size in sizes:
        for bit in bits_of(size):
            values = values + swap(values, axis, size, bit)
    return values


def layer(sizes):
    n_dp, n_mp = sizes
    far_bit = n_mp // 2
    dp_bits = bits_of(n_dp)

    def per_device(
        tokens,
        cotangent,
        segments,
        lengths,
        scale_levels,
        first_gain,
        first_shift,
        input_weight,
        input_bias,
        output_weight,
        output_bias,
        second_gain,
        second_shift,
        expand_weight,
        expand_bias,
        reduce_weight,
        reduce_bias,
    ):
        me = lax.axis_index("mp")
        group = lax.axis_index("dp")
        own_count, width = tokens.shape
        local_width = input_weight.shape[2]
        half_count = own_count * n_mp // 2
        item_blocks = [
            lax.dynamic_slice_in_dim(segments, (me ^ j) * own_count, own_count)
            for j in range(n_mp)
        ]
        positions, valid_rows = position_rows(
            item_blocks[0], lengths[0], scale_levels[0], me * own_count, width
        )
        residual = tokens.astype(F32) + positions
        normed_one, inverse_one = normalize(residual)
        attn_input = (normed_one * first_gain + first_shift).astype(BF16)
        grad_low = (cotangent.astype(F32) * valid_rows[:, None]).astype(BF16)

        far_own = swap(attn_input, "mp", n_mp, far_bit)
        attn_near = gather_near(attn_input, n_mp)
        far_own, grad_low = tie(far_own, grad_low)
        attn_far = gather_near(far_own, n_mp)
        grad_far = swap(grad_low, "mp", n_mp, far_bit)

        lanes = lax.broadcasted_iota(jnp.int32, (1, PAIR), 1)
        half_items = [
            jnp.concatenate(item_blocks[: n_mp // 2]),
            jnp.concatenate(item_blocks[n_mp // 2 :]),
        ]
        picks = [(items[:, None] == lanes).astype(BF16) for items in half_items]
        bars = [
            jnp.where(items[:, None] == lanes, 0.0, EXCLUDED).astype(BF16) for items in half_items
        ]
        bias_rows = jnp.stack([input_bias[0], jnp.zeros_like(input_bias[0]), input_bias[1]])

        def project(rows):
            wide = jnp.einsum("rd,tde->tre", rows, input_weight, preferred_element_type=F32)
            return (wide + bias_rows[:, None, :]).astype(BF16)

        qkv = [project(attn_near), project(attn_far)]
        query = [rows[0:1] for rows in qkv]
        keys = [rows[1:2] for rows in qkv]
        values = [rows[2:3] for rows in qkv]

        heads_far, logs_far = attend_forward(query[1], picks[1], keys, values, bars)
        share_far = dot_nn(heads_far, output_weight).astype(BF16)
        share_far, grad_far = tie(share_far, grad_far)
        sum_far = scatter_near(share_far, n_mp).astype(BF16)
        arrived = swap(sum_far, "mp", n_mp, far_bit)
        heads_near, logs_near = attend_forward(query[0], picks[0], keys, values, bars)
        share_near = dot_nn(heads_near, output_weight).astype(BF16)
        sum_near = scatter_near(share_near, n_mp)
        grad_near = gather_near(grad_low, n_mp)
        grad_far = gather_near(grad_far, n_mp)
        hidden_res = residual + (sum_near + arrived.astype(F32)) + output_bias
        normed_two, inverse_two = normalize(hidden_res)
        mlp_input = (normed_two * second_gain + second_shift).astype(BF16)

        far_own = swap(mlp_input, "mp", n_mp, far_bit)
        mlp_near = gather_near(mlp_input, n_mp)
        act_near, slope_near, back_near = mlp_both(
            mlp_near, grad_near, expand_weight, expand_bias, reduce_weight
        )
        mlp_far = gather_near(far_own, n_mp)
        act_far, slope_far, back_far = mlp_both(
            mlp_far, grad_far, expand_weight, expand_bias, reduce_weight
        )
        sum_far = scatter_near(back_far, n_mp).astype(BF16)
        arrived = swap(sum_far, "mp", n_mp, far_bit)
        sum_near = scatter_near(back_near, n_mp)

        activated = jnp.concatenate([act_near, act_far])
        pre_grad = jnp.concatenate([slope_near, slope_far])
        grad_all = jnp.concatenate([grad_near, grad_far])
        mlp_rows = jnp.concatenate([mlp_near, mlp_far])
        reduce_sum = DpSum(n_dp, group, dp_bits)
        expand_sum = DpSum(n_dp, group, dp_bits[1:] + dp_bits[:1])
        reduce_send = reduce_sum.open(activated, grad_all)
        expand_send = expand_sum.open(mlp_rows, pre_grad)
        reduce_in = reduce_sum.pass_on(reduce_send, reduce_sum.order[0])
        expand_in = expand_sum.pass_on(expand_send, expand_sum.order[0])

        normed_grad_two = sum_near + arrived.astype(F32)
        grad_out = grad_low.astype(F32)
        residual_grad = grad_out + normalize_back(
            normed_grad_two, normed_two, inverse_two, second_gain
        )
        branch_grad = residual_grad.astype(BF16)
        far_own = swap(branch_grad, "mp", n_mp, far_bit)
        branch_near = gather_near(branch_grad, n_mp)
        head_near = dot_nt(branch_near, output_weight).astype(BF16)
        query_near, key_part, value_part = attend_back(
            query[0], picks[0], head_near, heads_near, logs_near, keys, values, bars, None, False
        )
        share_far = dot_nn(act_far, reduce_weight).astype(BF16)
        share_near = dot_nn(act_near, reduce_weight).astype(BF16)
        far_own, share_far, reduce_in, expand_in = tie(far_own, share_far, reduce_in, expand_in)
        branch_far = gather_near(far_own, n_mp)
        head_far = dot_nt(branch_far, output_weight).astype(BF16)
        out_far = swap(scatter_near(share_far, n_mp).astype(BF16), "mp", n_mp, far_bit)
        out_near = scatter_near(share_near, n_mp)
        query_far, key_grads, value_grads = attend_back(
            query[1],
            picks[1],
            head_far,
            heads_far,
            logs_far,
            keys,
            values,
            bars,
            (key_part, value_part),
            True,
        )
        reduce_sum.add(reduce_in)
        expand_sum.add(expand_in)

        qkv_near = jnp.concatenate([query_near, key_grads[0], value_grads[0]], 1)
        qkv_far = jnp.concatenate([query_far, key_grads[1], value_grads[1]], 1)
        weight_wide = jnp.concatenate([input_weight[0], input_weight[1], input_weight[2]], 1)
        share_far = dot_nt(qkv_far, weight_wide).astype(BF16)
        share_far, out_far = tie(share_far, out_far)
        sum_far = scatter_near(share_far, n_mp).astype(BF16)
        arrived = swap(sum_far, "mp", n_mp, far_bit)
        sum_near = scatter_near(dot_nt(qkv_near, weight_wide).astype(BF16), n_mp)
        block_output = (hidden_res + (out_near + out_far.astype(F32)) + reduce_bias).astype(BF16)

        qkv_all = jnp.concatenate([qkv_near, qkv_far])
        attn_rows = jnp.concatenate([attn_near, attn_far])
        branch_all = jnp.concatenate([branch_near, branch_far])
        heads_all = jnp.concatenate([heads_near, heads_far])
        output_sum = DpSum(n_dp, group, dp_bits)
        input_sum = DpSum(n_dp, group, dp_bits)
        output_sum.add(output_sum.pass_on(output_sum.open(heads_all, branch_all), dp_bits[0]))
        input_sum.add(input_sum.pass_on(input_sum.open(attn_rows, qkv_all), dp_bits[0]))

        normed_grad_one = sum_near + arrived.astype(F32)
        input_gradient = residual_grad + normalize_back(
            normed_grad_one, normed_one, inverse_one, first_gain
        )
        reduce_sum.halve_rest()
        expand_sum.halve_rest()
        reduce_grad = reduce_sum.double_all()
        expand_grad = expand_sum.double_all()
        output_sum.halve_rest()
        input_sum.halve_rest()
        output_grad = output_sum.double_all()
        input_grad = input_sum.double_all()

        both = (("mp", n_mp), ("dp", n_dp))
        dp_only = (("dp", n_dp),)
        early = butterfly(
            jnp.stack(
                [
                    jnp.sum(normed_grad_two * normed_two, 0),
                    jnp.sum(normed_grad_two, 0),
                    jnp.sum(branch_grad, 0, dtype=F32),
                    jnp.sum(grad_out, 0),
                ]
            ),
            both,
        )
        hidden = expand_bias.shape[0]
        patches = jnp.sum(lengths).astype(F32)
        local = butterfly(
            jnp.concatenate([jnp.sum(pre_grad, 0, dtype=F32), jnp.full((PAIR,), patches)])[None],
            dp_only,
        )[0]
        factor = lax.rsqrt(local[hidden])
        late = butterfly(
            jnp.stack([jnp.sum(normed_grad_one * normed_one, 0), jnp.sum(normed_grad_one, 0)]),
            both,
        )
        wide_sums = jnp.sum(qkv_all, 0, dtype=F32)
        qv_total = butterfly(
            jnp.stack([wide_sums[:local_width], wide_sums[2 * local_width :]]), dp_only
        )
        input_total = input_grad.astype(F32) * factor
        return (
            block_output,
            input_gradient,
            late[0] * factor,
            late[1] * factor,
            jnp.stack(
                [input_total[:, t * local_width : (t + 1) * local_width] for t in range(3)]
            ),
            qv_total * factor,
            output_grad.astype(F32) * factor,
            early[2] * factor,
            early[0] * factor,
            early[1] * factor,
            expand_grad.astype(F32) * factor,
            local[:hidden] * factor,
            reduce_grad.astype(F32) * factor,
            early[3] * factor,
        )

    return per_device


def solution(mesh):
    placed = (
        P(("dp", "mp"), None),
        P(("dp", "mp"), None),
        P("dp"),
        P("dp", None),
        P("dp"),
        P(),
        P(),
        P(None, None, "mp"),
        P(None, "mp"),
        P("mp", None),
        P(),
        P(),
        P(),
        P(None, "mp"),
        P("mp"),
        P("mp", None),
        P(),
    )
    return jax.shard_map(
        layer((mesh.shape["dp"], mesh.shape["mp"])),
        mesh=mesh,
        in_specs=placed,
        out_specs=(
            P(("dp", "mp"), None),
            P(("dp", "mp"), None),
            P(),
            P(),
            P(None, None, "mp"),
            P(None, "mp"),
            P("mp", None),
            P(),
            P(),
            P(),
            P(None, "mp"),
            P("mp"),
            P("mp", None),
            P(),
        ),
        check_vma=False,
    )
```

```python
import functools
import jax
import jax.numpy as jnp
from jax import lax
from jax.experimental import pallas as pl
from jax.experimental.pallas import tpu as pltpu
from jax.sharding import PartitionSpec as P

F32 = jnp.float32
BF16 = jnp.bfloat16
PAIR = 128
HD = 64
EXCLUDED = -1e30
LIGHT = pl.CostEstimate(flops=1024, bytes_accessed=1024, transcendentals=0)


def dot_nn(a, b):
    return lax.dot_general(a, b, (((1,), (0,)), ((), ())), preferred_element_type=F32)


def dot_nt(a, b):
    return lax.dot_general(a, b, (((1,), (1,)), ((), ())), preferred_element_type=F32)


def dot_tn(a, b):
    return lax.dot_general(a, b, (((0,), (0,)), ((), ())), preferred_element_type=F32)


def head_lanes(head):
    lane = lax.broadcasted_iota(jnp.int32, (1, PAIR), 1)
    return (lane >= head * HD) & (lane < (head + 1) * HD)


def attend_kernel(halves, q_ref, pick_ref, *refs):
    k_refs, v_refs, bar_refs = (
        refs[:halves],
        refs[halves : 2 * halves],
        refs[2 * halves : 3 * halves],
    )
    out_ref, log_ref = refs[3 * halves :]
    scaled = q_ref[...] * jnp.asarray(HD**-0.5, BF16)
    pick = pick_ref[...]
    keys = [jnp.concatenate([k[...], b[...]], 1) for k, b in zip(k_refs, bar_refs)]
    rows = []
    for head in range(2):
        own = jnp.where(head_lanes(head), scaled, jnp.zeros_like(scaled))
        probe = jnp.concatenate([own, pick], 1)
        scores = [dot_nt(k, probe) for k in keys]
        top = functools.reduce(
            jnp.maximum, [jnp.max(s, 0, keepdims=True) for s in scores]
        )
        powers = [jnp.exp(s - top) for s in scores]
        total = functools.reduce(
            jnp.add, [jnp.sum(p, 0, keepdims=True) for p in powers]
        )
        summed = functools.reduce(
            jnp.add, [dot_tn(v[...], p.astype(BF16)) for v, p in zip(v_refs, powers)]
        )
        rows.append((summed / total)[head * HD : (head + 1) * HD])
        log_ref[0, head : head + 1, :] = top + jnp.log(total)
    out_ref[...] = jnp.concatenate(rows, 0).T.astype(BF16)


def attend_forward(own, pick, halves, bars, tile=256):
    count = own.shape[0]
    width = own.shape[1] // 3
    pairs = width // PAIR
    tile = min(tile, count)
    key_spec = [pl.BlockSpec((h.shape[0], PAIR), lambda p, i: (0, pairs + p)) for h in halves]
    value_spec = [pl.BlockSpec((h.shape[0], PAIR), lambda p, i: (0, 2 * pairs + p)) for h in halves]
    bar_spec = [pl.BlockSpec((b.shape[0], PAIR), lambda p, i: (0, 0)) for b in bars]
    total_keys = sum(h.shape[0] for h in halves)
    return pl.pallas_call(
        functools.partial(attend_kernel, len(halves)),
        grid=(pairs, count // tile),
        in_specs=[
            pl.BlockSpec((tile, PAIR), lambda p, i: (i, p)),
            pl.BlockSpec((tile, PAIR), lambda p, i: (i, 0)),
            *key_spec,
            *value_spec,
            *bar_spec,
        ],
        out_specs=[
            pl.BlockSpec((tile, PAIR), lambda p, i: (i, p)),
            pl.BlockSpec((1, 8, tile), lambda p, i: (p, 0, i)),
        ],
        out_shape=[
            jax.ShapeDtypeStruct((count, width), BF16),
            jax.ShapeDtypeStruct((pairs, 8, count), F32),
        ],
        cost_estimate=LIGHT,
        compiler_params=pltpu.CompilerParams(vmem_limit_bytes=24 * 2**20),
        name="attend_forward",
    )(own, pick, *halves, *halves, *bars)


def attend_back_kernel(halves, first, last, q_ref, pick_ref, grad_ref, out_ref, log_ref, *refs):
    k_refs, v_refs, bar_refs = (
        refs[:halves],
        refs[halves : 2 * halves],
        refs[2 * halves : 3 * halves],
    )
    rest = refs[3 * halves :]
    if not first:
        k_in, v_in = rest[:halves], rest[halves : 2 * halves]
        rest = rest[2 * halves :]
    q_grad_ref = rest[0]
    k_out, v_out = rest[1 : 1 + halves], rest[1 + halves : 1 + 2 * halves]
    if last:
        k_sum, v_sum = (
            rest[1 + 2 * halves : 1 + 3 * halves],
            rest[1 + 3 * halves : 1 + 4 * halves],
        )
    else:
        k_sum, v_sum = k_out, v_out
    step = pl.program_id(1)

    @pl.when(step == 0)
    def _():
        for n in range(halves):
            if first:
                k_sum[n][...] = jnp.zeros_like(k_sum[n])
                v_sum[n][...] = jnp.zeros_like(v_sum[n])
            else:
                k_sum[n][...] = k_in[n][...]
                v_sum[n][...] = v_in[n][...]

    scaled = q_ref[...] * jnp.asarray(HD**-0.5, BF16)
    grad = grad_ref[...]
    pick = pick_ref[...]
    both = (grad.astype(F32) * out_ref[...].astype(F32)).T
    owns = [jnp.where(head_lanes(h), scaled, jnp.zeros_like(scaled)) for h in range(2)]
    grads = [jnp.where(head_lanes(h), grad, jnp.zeros_like(grad)) for h in range(2)]
    probes = [jnp.concatenate([own, pick], 1) for own in owns]
    centers = [jnp.sum(both[h * HD : (h + 1) * HD], 0, keepdims=True) for h in range(2)]
    stacked_q = jnp.concatenate(owns, 0)
    stacked_g = jnp.concatenate(grads, 0)
    q_parts = [0.0, 0.0]
    for n in range(halves):
        keys = k_refs[n][...]
        values = v_refs[n][...]
        wide = jnp.concatenate([keys, bar_refs[n][...]], 1)
        probs = []
        slopes = []
        for h in range(2):
            prob = jnp.exp(dot_nt(wide, probes[h]) - log_ref[0, h : h + 1, :])
            slope = (prob * (dot_nt(values, grads[h]) - centers[h])).astype(BF16)
            probs.append(prob.astype(BF16))
            slopes.append(slope)
            q_parts[h] = q_parts[h] + dot_tn(keys, slope)
        v_sum[n][...] += dot_nn(jnp.concatenate(probs, 1), stacked_g)
        k_sum[n][...] += dot_nn(jnp.concatenate(slopes, 1), stacked_q)
    rows = [q_parts[h][h * HD : (h + 1) * HD] * (HD**-0.5) for h in range(2)]
    q_grad_ref[...] = jnp.concatenate(rows, 0).T.astype(BF16)

    if last:

        @pl.when(step == pl.num_programs(1) - 1)
        def _():
            for n in range(halves):
                k_out[n][...] = k_sum[n][...].astype(BF16)
                v_out[n][...] = v_sum[n][...].astype(BF16)


def attend_back(own, pick, grad, out, logs, halves, bars, carried, last, tile=256):
    count = own.shape[0]
    width = own.shape[1] // 3
    pairs = width // PAIR
    tile = min(tile, count)
    first = carried is None
    key_spec = [pl.BlockSpec((h.shape[0], PAIR), lambda p, i: (0, pairs + p)) for h in halves]
    value_spec = [pl.BlockSpec((h.shape[0], PAIR), lambda p, i: (0, 2 * pairs + p)) for h in halves]
    bar_spec = [pl.BlockSpec((b.shape[0], PAIR), lambda p, i: (0, 0)) for b in bars]
    sum_spec = [pl.BlockSpec((h.shape[0], PAIR), lambda p, i: (0, p)) for h in halves]
    row_spec = pl.BlockSpec((tile, PAIR), lambda p, i: (i, p))
    sum_type = BF16 if last else F32
    sums = [jax.ShapeDtypeStruct((h.shape[0], width), sum_type) for h in halves]
    total_keys = sum(h.shape[0] for h in halves)
    scratch = []
    if last:
        scratch = [pltpu.VMEM((h.shape[0], PAIR), F32) for h in halves] * 2
    extra = [] if first else list(carried[0]) + list(carried[1])
    parts = len(halves)
    result = pl.pallas_call(
        functools.partial(attend_back_kernel, parts, first, last),
        grid=(pairs, count // tile),
        in_specs=[
            row_spec,
            pl.BlockSpec((tile, PAIR), lambda p, i: (i, 0)),
            row_spec,
            row_spec,
            pl.BlockSpec((1, 8, tile), lambda p, i: (p, 0, i)),
            *key_spec,
            *value_spec,
            *bar_spec,
            *([] if first else sum_spec * 2),
        ],
        out_specs=[row_spec, *sum_spec, *sum_spec],
        out_shape=[jax.ShapeDtypeStruct((count, width), BF16), *sums, *sums],
        scratch_shapes=scratch,
        cost_estimate=LIGHT,
        compiler_params=pltpu.CompilerParams(vmem_limit_bytes=24 * 2**20),
        name="attend_back",
    )(own, pick, grad, out, logs, *halves, *halves, *bars, *extra)
    return result[0], result[1 : 1 + parts], result[1 + parts :]


def mlp_kernel(x_ref, grad_ref, up_ref, bias_ref, down_ref, act_ref, slope_ref, back_ref):
    pre = dot_nn(x_ref[...], up_ref[...]) + bias_ref[...]
    upstream = dot_nt(grad_ref[...], down_ref[...])
    cdf = 0.5 + 0.5 * lax.erf(pre * (0.5**0.5))
    act_ref[...] = (pre * cdf).astype(BF16)
    density = jnp.exp(-0.5 * pre * pre) * 0.3989422804014327
    slope = (upstream * (cdf + pre * density)).astype(BF16)
    slope_ref[...] = slope
    back_ref[...] = dot_nt(slope, up_ref[...]).astype(BF16)


def mlp_both(x, grad, up, bias, down, tile=256):
    count, width = x.shape
    hidden = up.shape[1]
    tile = min(tile, count)
    whole = lambda i: (0, 0)
    return pl.pallas_call(
        mlp_kernel,
        grid=(count // tile,),
        in_specs=[
            pl.BlockSpec((tile, width), lambda i: (i, 0)),
            pl.BlockSpec((tile, width), lambda i: (i, 0)),
            pl.BlockSpec((width, hidden), whole, pipeline_mode=pl.Buffered(1)),
            pl.BlockSpec((1, hidden), whole),
            pl.BlockSpec((hidden, width), whole, pipeline_mode=pl.Buffered(1)),
        ],
        out_specs=[
            pl.BlockSpec((tile, hidden), lambda i: (i, 0)),
            pl.BlockSpec((tile, hidden), lambda i: (i, 0)),
            pl.BlockSpec((tile, width), lambda i: (i, 0)),
        ],
        out_shape=[
            jax.ShapeDtypeStruct((count, hidden), BF16),
            jax.ShapeDtypeStruct((count, hidden), BF16),
            jax.ShapeDtypeStruct((count, width), BF16),
        ],
        cost_estimate=LIGHT,
        compiler_params=pltpu.CompilerParams(vmem_limit_bytes=24 * 2**20),
        name="mlp_both",
    )(x, grad, up, bias[None], down)


EPSILON = 1e-06


def normalize(values):
    center = values - jnp.mean(values, -1, keepdims=True)
    inverse = lax.rsqrt(jnp.mean(center * center, -1, keepdims=True) + EPSILON)
    return (center * inverse, inverse)


def normalize_back(upstream, normed, inverse, gain):
    scaled = upstream * gain
    return inverse * (
        scaled
        - jnp.mean(scaled, -1, keepdims=True)
        - normed * jnp.mean(scaled * normed, -1, keepdims=True)
    )


def position_rows(own_items, item_lengths, level, first_row, width):
    slot_count = item_lengths.shape[0]
    slot_index = lax.broadcasted_iota(jnp.int32, (1, slot_count), 1)
    start_row = jnp.sum(jnp.where(slot_index < own_items[:, None], item_lengths[None, :], 0), 1)
    row_index = first_row + jnp.arange(own_items.shape[0], dtype=jnp.int32)
    valid_rows = (own_items < slot_count).astype(F32)
    level_ratio = jnp.exp2(level.astype(F32) - 2.0)
    places = (row_index - start_row).astype(F32) * level_ratio
    half_width = width // 2
    frequency = jnp.exp(-jnp.log(10000.0) * jnp.arange(half_width, dtype=F32) / half_width)
    angles = places[:, None] * frequency[None, :]
    return (
        jnp.concatenate([jnp.sin(angles), jnp.cos(angles)], 1) * valid_rows[:, None],
        valid_rows,
    )


def bits_of(size):
    bits = []
    step = 1
    while step < size:
        bits.append(step)
        step *= 2
    return bits


def tie(*arrays):
    return lax.optimization_barrier(arrays)


def swap(array, axis, size, bit):
    return lax.ppermute(array, axis, [(i, i ^ bit) for i in range(size)])


def gather_near(own, count):
    blocks = {0: own}
    for bit in reversed(bits_of(count)[:-1]):
        blocks.update(
            {j | bit: swap(rows, "mp", count, bit) for j, rows in list(blocks.items())}
        )
    return jnp.concatenate([blocks[j] for j in range(count // 2)])


def scatter_near(rows, count):
    size = rows.shape[0] // (count // 2)
    held = {j: rows[j * size : (j + 1) * size] for j in range(count // 2)}
    for bit in bits_of(count)[:-1]:
        arrived = {
            j ^ bit: swap(held[j].astype(BF16), "mp", count, bit) for j in held if j & bit
        }
        held = {j: held[j].astype(F32) + arrived[j].astype(F32) for j in arrived}
    return held[0]


class DpSum:
    def __init__(self, count, index, order):
        self.count, self.index = count, index
        self.order = order
        self.steps = list(order) + list(reversed(order))
        self.at = 0

    def high(self, bit):
        return (self.index & bit) != 0

    def open(self, pairs):
        half = pairs[0][0].shape[1] // 2
        top = jnp.where(self.high(self.order[0]), half, 0)

        def part(start):
            dots = [
                dot_tn(lax.dynamic_slice_in_dim(left, start, half, 1), right)
                for left, right in pairs
            ]
            return functools.reduce(jnp.add, dots).astype(BF16)

        self.send = part(half - top)
        self.held = part(top)

    def launch(self):
        self.flying = swap(self.send, "dp", self.count, self.steps[self.at])

    def land(self):
        bit = self.steps[self.at]
        if self.at < len(self.order):
            self.held = (self.held.astype(F32) + self.flying.astype(F32)).astype(BF16)
        else:
            self.held = jnp.where(
                self.high(bit),
                jnp.concatenate([self.flying, self.held]),
                jnp.concatenate([self.held, self.flying]),
            )
        self.at += 1
        if self.at < len(self.order):
            half = self.held.shape[0] // 2
            top = jnp.where(self.high(self.steps[self.at]), half, 0)
            self.send = lax.dynamic_slice_in_dim(self.held, half - top, half, 0)
            self.held = lax.dynamic_slice_in_dim(self.held, top, half, 0)
        else:
            self.send = self.held

    def busy(self):
        return self.at < len(self.steps)


class SmallSum:
    def __init__(self, count, order, values):
        self.count, self.steps, self.at = count, list(order), 0
        self.send = self.held = values

    def launch(self):
        self.held = self.send
        self.flying = swap(self.send, "dp", self.count, self.steps[self.at])

    def land(self):
        self.send = self.held = self.held + self.flying
        self.at += 1

    def busy(self):
        return self.at < len(self.steps)


def await_all(chain, sums):
    tied = tie(*chain, *[s.flying for s in sums])
    for s, value in zip(sums, tied[len(chain) :]):
        s.flying = value
        s.land()
    return tied[: len(chain)]


def start_all(chain, sums):
    sums = [s for s in sums if s.busy()]
    tied = tie(*chain, *[s.send for s in sums])
    for s, value in zip(sums, tied[len(chain) :]):
        s.send = value
        s.launch()
    return tied[: len(chain)]


def butterfly(values, sizes):
    for axis, size in sizes:
        for bit in bits_of(size):
            values = values + swap(values, axis, size, bit)
    return values


def layer(sizes):
    n_dp, n_mp = sizes
    far_bit = n_mp // 2
    dp_bits = bits_of(n_dp)

    def per_device(
        tokens,
        cotangent,
        segments,
        lengths,
        scale_levels,
        first_gain,
        first_shift,
        input_weight,
        input_bias,
        output_weight,
        output_bias,
        second_gain,
        second_shift,
        expand_weight,
        expand_bias,
        reduce_weight,
        reduce_bias,
    ):
        me = lax.axis_index("mp")
        group = lax.axis_index("dp")
        own_count, width = tokens.shape
        local_width = input_weight.shape[2]
        half_count = own_count * n_mp // 2
        item_blocks = [
            lax.dynamic_slice_in_dim(segments, (me ^ j) * own_count, own_count)
            for j in range(n_mp)
        ]
        positions, valid_rows = position_rows(
            item_blocks[0], lengths[0], scale_levels[0], me * own_count, width
        )
        residual = tokens.astype(F32) + positions
        normed_one, inverse_one = normalize(residual)
        attn_input = (normed_one * first_gain + first_shift).astype(BF16)
        grad_low = (cotangent.astype(F32) * valid_rows[:, None]).astype(BF16)

        far_own = swap(attn_input, "mp", n_mp, far_bit)
        attn_near = gather_near(attn_input, n_mp)
        lanes = lax.broadcasted_iota(jnp.int32, (1, PAIR), 1)
        half_items = [
            jnp.concatenate(item_blocks[: n_mp // 2]),
            jnp.concatenate(item_blocks[n_mp // 2 :]),
        ]
        picks = [(items[:, None] == lanes).astype(BF16) for items in half_items]
        bars = [
            jnp.where(items[:, None] == lanes, 0.0, EXCLUDED).astype(BF16) for items in half_items
        ]
        bias_wide = jnp.concatenate([input_bias[0], jnp.zeros_like(input_bias[0]), input_bias[1]])
        weight_wide = jnp.concatenate([input_weight[0], input_weight[1], input_weight[2]], 1)

        def project(rows):
            return (dot_nn(rows, weight_wide) + bias_wide).astype(BF16)

        near = project(attn_near)
        far_own, near, grad_low = tie(far_own, near, grad_low)
        attn_far = gather_near(far_own, n_mp)
        grad_far = swap(grad_low, "mp", n_mp, far_bit)
        far = project(attn_far)

        heads_far, logs_far = attend_forward(far, picks[1], [near, far], bars)
        share_far = dot_nn(heads_far, output_weight).astype(BF16)
        sum_far = scatter_near(share_far, n_mp).astype(BF16)
        sum_far, near = tie(sum_far, near)
        arrived = swap(sum_far, "mp", n_mp, far_bit)
        heads_near, logs_near = attend_forward(near, picks[0], [near, far], bars)
        share_near = dot_nn(heads_near, output_weight).astype(BF16)
        sum_near = scatter_near(share_near, n_mp)
        grad_near = gather_near(grad_low, n_mp)
        grad_far = gather_near(grad_far, n_mp)
        arrived, grad_near, grad_far = tie(arrived, grad_near, grad_far)
        hidden_res = residual + (sum_near + arrived.astype(F32)) + output_bias
        normed_two, inverse_two = normalize(hidden_res)
        mlp_input = (normed_two * second_gain + second_shift).astype(BF16)

        far_own = swap(mlp_input, "mp", n_mp, far_bit)
        mlp_near = gather_near(mlp_input, n_mp)
        act_near, slope_near, back_near = mlp_both(
            mlp_near, grad_near, expand_weight, expand_bias, reduce_weight
        )
        share_near = dot_nn(act_near, reduce_weight).astype(BF16)
        sum_near = scatter_near(back_near, n_mp)
        far_own, sum_near, share_near = tie(far_own, sum_near, share_near)
        mlp_far = gather_near(far_own, n_mp)
        act_far, slope_far, back_far = mlp_both(
            mlp_far, grad_far, expand_weight, expand_bias, reduce_weight
        )
        swapped = dp_bits[1:2] + dp_bits[:1] + dp_bits[2:]
        reduce_sum = DpSum(n_dp, group, dp_bits)
        expand_sum = DpSum(n_dp, group, swapped)
        output_sum = DpSum(n_dp, group, dp_bits)
        input_sum = DpSum(n_dp, group, dp_bits)
        reduce_sum.open([(act_near, grad_near), (act_far, grad_far)])
        sum_far = scatter_near(back_far, n_mp).astype(BF16)
        sum_far, slope_near, slope_far = start_all((sum_far, slope_near, slope_far), [reduce_sum])
        arrived = swap(sum_far, "mp", n_mp, far_bit)
        expand_sum.open([(mlp_near, slope_near), (mlp_far, slope_far)])
        (sum_near,) = start_all((sum_near,), [expand_sum])
        share_far = dot_nn(act_far, reduce_weight).astype(BF16)
        arrived, share_far, reduce_sum.held, expand_sum.held = tie(
            arrived, share_far, reduce_sum.held, expand_sum.held
        )

        normed_grad_two = sum_near + arrived.astype(F32)
        grad_out = grad_low.astype(F32)
        residual_grad = grad_out + normalize_back(
            normed_grad_two, normed_two, inverse_two, second_gain
        )
        branch_grad = residual_grad.astype(BF16)
        far_own = swap(branch_grad, "mp", n_mp, far_bit)
        branch_near = gather_near(branch_grad, n_mp)
        out_sum = scatter_near(share_far, n_mp).astype(BF16)
        branch_near, out_sum = tie(branch_near, out_sum)
        out_far = swap(out_sum, "mp", n_mp, far_bit)
        head_near = dot_nt(branch_near, output_weight).astype(BF16)
        query_near, key_part, value_part = attend_back(
            near, picks[0], head_near, heads_near, logs_near, [near, far], bars, None, False
        )
        out_near = scatter_near(share_near, n_mp)
        over_mp = (("mp", n_mp),)
        early = butterfly(
            jnp.stack(
                [
                    jnp.sum(normed_grad_two * normed_two, 0),
                    jnp.sum(normed_grad_two, 0),
                    jnp.sum(branch_grad, 0, dtype=F32),
                    jnp.sum(grad_out, 0),
                ]
            ),
            over_mp,
        )
        far_own, query_near = await_all((far_own, query_near), [reduce_sum, expand_sum])
        branch_far = gather_near(far_own, n_mp)
        (branch_far,) = start_all((branch_far,), [reduce_sum, expand_sum])
        output_sum.open([(heads_near, branch_near), (heads_far, branch_far)])
        head_far = dot_nt(branch_far, output_weight).astype(BF16)
        head_far, out_near, early = start_all((head_far, out_near, early), [output_sum])
        query_far, key_grads, value_grads = attend_back(
            far,
            picks[1],
            head_far,
            heads_far,
            logs_far,
            [near, far],
            bars,
            (key_part, value_part),
            True,
        )

        qkv_near = jnp.concatenate([query_near, key_grads[0], value_grads[0]], 1)
        qkv_far = jnp.concatenate([query_far, key_grads[1], value_grads[1]], 1)
        input_sum.open([(attn_near, qkv_near), (attn_far, qkv_far)])
        share_far = dot_nt(qkv_far, weight_wide).astype(BF16)
        sum_far = scatter_near(share_far, n_mp).astype(BF16)
        (sum_far,) = start_all((sum_far,), [input_sum])
        arrived = swap(sum_far, "mp", n_mp, far_bit)
        sum_near = scatter_near(dot_nt(qkv_near, weight_wide).astype(BF16), n_mp)
        sum_near, input_sum.held = await_all(
            (sum_near, input_sum.held), [reduce_sum, expand_sum]
        )
        (sum_near,) = start_all((sum_near,), [reduce_sum, expand_sum])
        (arrived,) = await_all((arrived,), [output_sum])
        arrived, sum_near, out_far = start_all((arrived, sum_near, out_far), [output_sum])
        block_output = (hidden_res + (out_near + out_far.astype(F32)) + reduce_bias).astype(BF16)
        normed_grad_one = sum_near + arrived.astype(F32)
        input_gradient = residual_grad + normalize_back(
            normed_grad_one, normed_one, inverse_one, first_gain
        )
        late = butterfly(
            jnp.stack([jnp.sum(normed_grad_one * normed_one, 0), jnp.sum(normed_grad_one, 0)]),
            over_mp,
        )
        hidden = expand_bias.shape[0]
        hidden_sums = jnp.sum(slope_near, 0, dtype=F32) + jnp.sum(slope_far, 0, dtype=F32)
        wide_sums = jnp.sum(qkv_near, 0, dtype=F32) + jnp.sum(qkv_far, 0, dtype=F32)
        small = SmallSum(
            n_dp,
            dp_bits,
            jnp.concatenate(
                [
                    early.reshape(-1),
                    late.reshape(-1),
                    wide_sums[:local_width],
                    wide_sums[2 * local_width :],
                    hidden_sums,
                    jnp.full((PAIR,), jnp.sum(lengths).astype(F32)),
                ]
            ),
        )
        (block_output,) = start_all((block_output,), [small])
        sums = [input_sum, small, output_sum, reduce_sum, expand_sum]
        token = block_output
        while any(s.busy() for s in sums):
            for s in sums:
                if s.busy():
                    (token,) = await_all((token,), [s])
                    (token,) = start_all((token,), [s])
        block_output = token

        total = small.held
        rows = total[: 6 * width].reshape(6, width)
        rest = total[6 * width :]
        factor = lax.rsqrt(rest[2 * local_width + hidden])
        rows = rows * factor
        input_total = input_sum.held.astype(F32) * factor
        return (
            block_output,
            input_gradient,
            rows[4],
            rows[5],
            jnp.stack(
                [input_total[:, t * local_width : (t + 1) * local_width] for t in range(3)]
            ),
            rest[: 2 * local_width].reshape(2, local_width) * factor,
            output_sum.held.astype(F32) * factor,
            rows[2],
            rows[0],
            rows[1],
            expand_sum.held.astype(F32) * factor,
            rest[2 * local_width : 2 * local_width + hidden] * factor,
            reduce_sum.held.astype(F32) * factor,
            rows[3],
        )
    return per_device


def solution(mesh):
    placed = (
        P(("dp", "mp"), None),
        P(("dp", "mp"), None),
        P("dp"),
        P("dp", None),
        P("dp"),
        P(),
        P(),
        P(None, None, "mp"),
        P(None, "mp"),
        P("mp", None),
        P(),
        P(),
        P(),
        P(None, "mp"),
        P("mp"),
        P("mp", None),
        P(),
    )
    return jax.shard_map(
        layer((mesh.shape["dp"], mesh.shape["mp"])),
        mesh=mesh,
        in_specs=placed,
        out_specs=(
            P(("dp", "mp"), None),
            P(("dp", "mp"), None),
            P(),
            P(),
            P(None, None, "mp"),
            P(None, "mp"),
            P("mp", None),
            P(),
            P(),
            P(),
            P(None, "mp"),
            P("mp"),
            P("mp", None),
            P(),
        ),
        check_vma=False,
    )
```

```python
import functools
import jax
import jax.numpy as jnp
from jax import lax
from jax.experimental import pallas as pl
from jax.experimental.pallas import tpu as pltpu
from jax.sharding import PartitionSpec as P

F32 = jnp.float32
BF16 = jnp.bfloat16
PAIR = 128
HD = 64
EXCLUDED = -1e30
LIGHT = pl.CostEstimate(flops=1024, bytes_accessed=1024, transcendentals=0)


def dot_nn(a, b):
    return lax.dot_general(a, b, (((1,), (0,)), ((), ())), preferred_element_type=F32)


def dot_nt(a, b):
    return lax.dot_general(a, b, (((1,), (1,)), ((), ())), preferred_element_type=F32)


def dot_tn(a, b):
    return lax.dot_general(a, b, (((0,), (0,)), ((), ())), preferred_element_type=F32)


def head_lanes(head):
    lane = lax.broadcasted_iota(jnp.int32, (1, PAIR), 1)
    return (lane >= head * HD) & (lane < (head + 1) * HD)


def attend_kernel(halves, q_ref, pick_ref, *refs):
    k_refs, v_refs, bar_refs = (
        refs[:halves],
        refs[halves : 2 * halves],
        refs[2 * halves : 3 * halves],
    )
    out_ref, log_ref = refs[3 * halves :]
    scaled = q_ref[...] * jnp.asarray(HD**-0.5, BF16)
    pick = pick_ref[...]
    keys = [jnp.concatenate([k[...], b[...]], 1) for k, b in zip(k_refs, bar_refs)]
    rows = []
    for head in range(2):
        own = jnp.where(head_lanes(head), scaled, jnp.zeros_like(scaled))
        probe = jnp.concatenate([own, pick], 1)
        scores = [dot_nt(k, probe) for k in keys]
        top = functools.reduce(
            jnp.maximum, [jnp.max(s, 0, keepdims=True) for s in scores]
        )
        powers = [jnp.exp(s - top) for s in scores]
        total = functools.reduce(
            jnp.add, [jnp.sum(p, 0, keepdims=True) for p in powers]
        )
        summed = functools.reduce(
            jnp.add, [dot_tn(v[...], p.astype(BF16)) for v, p in zip(v_refs, powers)]
        )
        rows.append((summed / total)[head * HD : (head + 1) * HD])
        log_ref[0, head : head + 1, :] = top + jnp.log(total)
    out_ref[...] = jnp.concatenate(rows, 0).T.astype(BF16)


def attend_forward(own, pick, halves, bars, tile=256):
    count = own.shape[0]
    width = own.shape[1] // 3
    pairs = width // PAIR
    tile = min(tile, count)
    key_spec = [pl.BlockSpec((h.shape[0], PAIR), lambda p, i: (0, pairs + p)) for h in halves]
    value_spec = [pl.BlockSpec((h.shape[0], PAIR), lambda p, i: (0, 2 * pairs + p)) for h in halves]
    bar_spec = [pl.BlockSpec((b.shape[0], PAIR), lambda p, i: (0, 0)) for b in bars]
    total_keys = sum(h.shape[0] for h in halves)
    return pl.pallas_call(
        functools.partial(attend_kernel, len(halves)),
        grid=(pairs, count // tile),
        in_specs=[
            pl.BlockSpec((tile, PAIR), lambda p, i: (i, p)),
            pl.BlockSpec((tile, PAIR), lambda p, i: (i, 0)),
            *key_spec,
            *value_spec,
            *bar_spec,
        ],
        out_specs=[
            pl.BlockSpec((tile, PAIR), lambda p, i: (i, p)),
            pl.BlockSpec((1, 8, tile), lambda p, i: (p, 0, i)),
        ],
        out_shape=[
            jax.ShapeDtypeStruct((count, width), BF16),
            jax.ShapeDtypeStruct((pairs, 8, count), F32),
        ],
        cost_estimate=LIGHT,
        compiler_params=pltpu.CompilerParams(vmem_limit_bytes=24 * 2**20),
        name="attend_forward",
    )(own, pick, *halves, *halves, *bars)


def attend_back_kernel(halves, first, last, q_ref, pick_ref, grad_ref, out_ref, log_ref, *refs):
    k_refs, v_refs, bar_refs = (
        refs[:halves],
        refs[halves : 2 * halves],
        refs[2 * halves : 3 * halves],
    )
    rest = refs[3 * halves :]
    if not first:
        k_in, v_in = rest[:halves], rest[halves : 2 * halves]
        rest = rest[2 * halves :]
    q_grad_ref = rest[0]
    k_out, v_out = rest[1 : 1 + halves], rest[1 + halves : 1 + 2 * halves]
    if last:
        k_sum, v_sum = (
            rest[1 + 2 * halves : 1 + 3 * halves],
            rest[1 + 3 * halves : 1 + 4 * halves],
        )
    else:
        k_sum, v_sum = k_out, v_out
    step = pl.program_id(1)

    @pl.when(step == 0)
    def _():
        for n in range(halves):
            if first:
                k_sum[n][...] = jnp.zeros_like(k_sum[n])
                v_sum[n][...] = jnp.zeros_like(v_sum[n])
            else:
                k_sum[n][...] = k_in[n][...]
                v_sum[n][...] = v_in[n][...]

    scaled = q_ref[...] * jnp.asarray(HD**-0.5, BF16)
    grad = grad_ref[...]
    pick = pick_ref[...]
    both = (grad.astype(F32) * out_ref[...].astype(F32)).T
    owns = [jnp.where(head_lanes(h), scaled, jnp.zeros_like(scaled)) for h in range(2)]
    grads = [jnp.where(head_lanes(h), grad, jnp.zeros_like(grad)) for h in range(2)]
    probes = [jnp.concatenate([own, pick], 1) for own in owns]
    centers = [jnp.sum(both[h * HD : (h + 1) * HD], 0, keepdims=True) for h in range(2)]
    stacked_q = jnp.concatenate(owns, 0)
    stacked_g = jnp.concatenate(grads, 0)
    q_parts = [0.0, 0.0]
    for n in range(halves):
        keys = k_refs[n][...]
        values = v_refs[n][...]
        wide = jnp.concatenate([keys, bar_refs[n][...]], 1)
        probs = []
        slopes = []
        for h in range(2):
            prob = jnp.exp(dot_nt(wide, probes[h]) - log_ref[0, h : h + 1, :])
            slope = (prob * (dot_nt(values, grads[h]) - centers[h])).astype(BF16)
            probs.append(prob.astype(BF16))
            slopes.append(slope)
            q_parts[h] = q_parts[h] + dot_tn(keys, slope)
        v_sum[n][...] += dot_nn(jnp.concatenate(probs, 1), stacked_g)
        k_sum[n][...] += dot_nn(jnp.concatenate(slopes, 1), stacked_q)
    rows = [q_parts[h][h * HD : (h + 1) * HD] * (HD**-0.5) for h in range(2)]
    q_grad_ref[...] = jnp.concatenate(rows, 0).T.astype(BF16)

    if last:

        @pl.when(step == pl.num_programs(1) - 1)
        def _():
            for n in range(halves):
                k_out[n][...] = k_sum[n][...].astype(BF16)
                v_out[n][...] = v_sum[n][...].astype(BF16)


def attend_back(own, pick, grad, out, logs, halves, bars, carried, last, tile=256):
    count = own.shape[0]
    width = own.shape[1] // 3
    pairs = width // PAIR
    tile = min(tile, count)
    first = carried is None
    key_spec = [pl.BlockSpec((h.shape[0], PAIR), lambda p, i: (0, pairs + p)) for h in halves]
    value_spec = [pl.BlockSpec((h.shape[0], PAIR), lambda p, i: (0, 2 * pairs + p)) for h in halves]
    bar_spec = [pl.BlockSpec((b.shape[0], PAIR), lambda p, i: (0, 0)) for b in bars]
    sum_spec = [pl.BlockSpec((h.shape[0], PAIR), lambda p, i: (0, p)) for h in halves]
    row_spec = pl.BlockSpec((tile, PAIR), lambda p, i: (i, p))
    sum_type = BF16 if last else F32
    sums = [jax.ShapeDtypeStruct((h.shape[0], width), sum_type) for h in halves]
    total_keys = sum(h.shape[0] for h in halves)
    scratch = []
    if last:
        scratch = [pltpu.VMEM((h.shape[0], PAIR), F32) for h in halves] * 2
    extra = [] if first else list(carried[0]) + list(carried[1])
    parts = len(halves)
    result = pl.pallas_call(
        functools.partial(attend_back_kernel, parts, first, last),
        grid=(pairs, count // tile),
        in_specs=[
            row_spec,
            pl.BlockSpec((tile, PAIR), lambda p, i: (i, 0)),
            row_spec,
            row_spec,
            pl.BlockSpec((1, 8, tile), lambda p, i: (p, 0, i)),
            *key_spec,
            *value_spec,
            *bar_spec,
            *([] if first else sum_spec * 2),
        ],
        out_specs=[row_spec, *sum_spec, *sum_spec],
        out_shape=[jax.ShapeDtypeStruct((count, width), BF16), *sums, *sums],
        scratch_shapes=scratch,
        cost_estimate=LIGHT,
        compiler_params=pltpu.CompilerParams(vmem_limit_bytes=24 * 2**20),
        name="attend_back",
    )(own, pick, grad, out, logs, *halves, *halves, *bars, *extra)
    return result[0], result[1 : 1 + parts], result[1 + parts :]


def mlp_kernel(x_ref, grad_ref, up_ref, bias_ref, down_ref, act_ref, slope_ref, back_ref):
    pre = dot_nn(x_ref[...], up_ref[...]) + bias_ref[...]
    upstream = dot_nt(grad_ref[...], down_ref[...])
    cdf = 0.5 + 0.5 * lax.erf(pre * (0.5**0.5))
    act_ref[...] = (pre * cdf).astype(BF16)
    density = jnp.exp(-0.5 * pre * pre) * 0.3989422804014327
    slope = (upstream * (cdf + pre * density)).astype(BF16)
    slope_ref[...] = slope
    back_ref[...] = dot_nt(slope, up_ref[...]).astype(BF16)


def mlp_both(x, grad, up, bias, down, tile=256):
    count, width = x.shape
    hidden = up.shape[1]
    tile = min(tile, count)
    whole = lambda i: (0, 0)
    return pl.pallas_call(
        mlp_kernel,
        grid=(count // tile,),
        in_specs=[
            pl.BlockSpec((tile, width), lambda i: (i, 0)),
            pl.BlockSpec((tile, width), lambda i: (i, 0)),
            pl.BlockSpec((width, hidden), whole, pipeline_mode=pl.Buffered(1)),
            pl.BlockSpec((1, hidden), whole),
            pl.BlockSpec((hidden, width), whole, pipeline_mode=pl.Buffered(1)),
        ],
        out_specs=[
            pl.BlockSpec((tile, hidden), lambda i: (i, 0)),
            pl.BlockSpec((tile, hidden), lambda i: (i, 0)),
            pl.BlockSpec((tile, width), lambda i: (i, 0)),
        ],
        out_shape=[
            jax.ShapeDtypeStruct((count, hidden), BF16),
            jax.ShapeDtypeStruct((count, hidden), BF16),
            jax.ShapeDtypeStruct((count, width), BF16),
        ],
        cost_estimate=LIGHT,
        compiler_params=pltpu.CompilerParams(vmem_limit_bytes=24 * 2**20),
        name="mlp_both",
    )(x, grad, up, bias[None], down)


EPSILON = 1e-06


def normalize(values):
    center = values - jnp.mean(values, -1, keepdims=True)
    inverse = lax.rsqrt(jnp.mean(center * center, -1, keepdims=True) + EPSILON)
    return (center * inverse, inverse)


def normalize_back(upstream, normed, inverse, gain):
    scaled = upstream * gain
    return inverse * (
        scaled
        - jnp.mean(scaled, -1, keepdims=True)
        - normed * jnp.mean(scaled * normed, -1, keepdims=True)
    )


def position_rows(own_items, item_lengths, level, first_row, width):
    slot_count = item_lengths.shape[0]
    slot_index = lax.broadcasted_iota(jnp.int32, (1, slot_count), 1)
    start_row = jnp.sum(jnp.where(slot_index < own_items[:, None], item_lengths[None, :], 0), 1)
    row_index = first_row + jnp.arange(own_items.shape[0], dtype=jnp.int32)
    valid_rows = (own_items < slot_count).astype(F32)
    level_ratio = jnp.exp2(level.astype(F32) - 2.0)
    places = (row_index - start_row).astype(F32) * level_ratio
    half_width = width // 2
    frequency = jnp.exp(-jnp.log(10000.0) * jnp.arange(half_width, dtype=F32) / half_width)
    angles = places[:, None] * frequency[None, :]
    return (
        jnp.concatenate([jnp.sin(angles), jnp.cos(angles)], 1) * valid_rows[:, None],
        valid_rows,
    )


def bits_of(size):
    bits = []
    step = 1
    while step < size:
        bits.append(step)
        step *= 2
    return bits


def tie(*arrays):
    return lax.optimization_barrier(arrays)


def swap(array, axis, size, bit):
    return lax.ppermute(array, axis, [(i, i ^ bit) for i in range(size)])


def gather_near(own, count):
    blocks = {0: own}
    for bit in reversed(bits_of(count)[:-1]):
        blocks.update(
            {j | bit: swap(rows, "mp", count, bit) for j, rows in list(blocks.items())}
        )
    return jnp.concatenate([blocks[j] for j in range(count // 2)])


def scatter_near(pieces, count):
    held = dict(enumerate(pieces))
    bits = bits_of(count)[:-1]
    for bit in bits:
        arrived = {
            j ^ bit: swap(held[j].astype(BF16), "mp", count, bit) for j in held if j & bit
        }
        if bit == bits[-1]:
            return held[0], arrived[0]
        held = {j: held[j].astype(F32) + arrived[j].astype(F32) for j in arrived}


def add_up(pair):
    return pair[0].astype(F32) + pair[1].astype(F32)


class DpSum:
    def __init__(self, count, index, order):
        self.count, self.index = count, index
        self.order = order
        self.steps = list(order) + list(reversed(order))
        self.at = 0

    def high(self, bit):
        return (self.index & bit) != 0

    def half(self, pairs, other):
        size = pairs[0][0].shape[1] // 2
        top = jnp.where(self.high(self.order[0]) != other, size, 0)
        dots = [
            dot_tn(lax.dynamic_slice_in_dim(left, top, size, 1), right) for left, right in pairs
        ]
        return functools.reduce(jnp.add, dots).astype(BF16)

    def open(self, pairs):
        self.send = self.half(pairs, True)

    def keep(self, pairs):
        self.held = self.half(pairs, False)

    def launch(self):
        self.flying = swap(self.send, "dp", self.count, self.steps[self.at])

    def land(self):
        bit = self.steps[self.at]
        if self.at < len(self.order):
            self.held = (self.held.astype(F32) + self.flying.astype(F32)).astype(BF16)
        else:
            self.held = jnp.where(
                self.high(bit),
                jnp.concatenate([self.flying, self.held]),
                jnp.concatenate([self.held, self.flying]),
            )
        self.at += 1
        if self.at < len(self.order):
            half = self.held.shape[0] // 2
            top = jnp.where(self.high(self.steps[self.at]), half, 0)
            self.send = lax.dynamic_slice_in_dim(self.held, half - top, half, 0)
            self.held = lax.dynamic_slice_in_dim(self.held, top, half, 0)
        else:
            self.send = self.held

    def busy(self):
        return self.at < len(self.steps)


class SmallSum:
    def __init__(self, count, order, values):
        self.count, self.steps, self.at = count, list(order), 0
        self.send = self.held = values

    def launch(self):
        self.held = self.send
        self.flying = swap(self.send, "dp", self.count, self.steps[self.at])

    def land(self):
        self.send = self.held = self.held + self.flying
        self.at += 1

    def busy(self):
        return self.at < len(self.steps)


def await_all(chain, sums):
    tied = tie(*chain, *[s.flying for s in sums])
    for s, value in zip(sums, tied[len(chain) :]):
        s.flying = value
        s.land()
    return tied[: len(chain)]


def start_all(chain, sums):
    sums = [s for s in sums if s.busy()]
    tied = tie(*chain, *[s.send for s in sums])
    for s, value in zip(sums, tied[len(chain) :]):
        s.send = value
        s.launch()
    return tied[: len(chain)]


def butterfly(values, sizes):
    for axis, size in sizes:
        for bit in bits_of(size):
            values = values + swap(values, axis, size, bit)
    return values


def layer(sizes):
    n_dp, n_mp = sizes
    far_bit = n_mp // 2
    dp_bits = bits_of(n_dp)

    def per_device(
        tokens,
        cotangent,
        segments,
        lengths,
        scale_levels,
        first_gain,
        first_shift,
        input_weight,
        input_bias,
        output_weight,
        output_bias,
        second_gain,
        second_shift,
        expand_weight,
        expand_bias,
        reduce_weight,
        reduce_bias,
    ):
        me = lax.axis_index("mp")
        group = lax.axis_index("dp")
        own_count, width = tokens.shape
        local_width = input_weight.shape[2]
        half_count = own_count * n_mp // 2
        item_blocks = [
            lax.dynamic_slice_in_dim(segments, (me ^ j) * own_count, own_count)
            for j in range(n_mp)
        ]
        positions, valid_rows = position_rows(
            item_blocks[0], lengths[0], scale_levels[0], me * own_count, width
        )
        residual = tokens.astype(F32) + positions
        normed_one, inverse_one = normalize(residual)
        attn_input = (normed_one * first_gain + first_shift).astype(BF16)
        grad_low = (cotangent.astype(F32) * valid_rows[:, None]).astype(BF16)

        far_own = swap(attn_input, "mp", n_mp, far_bit)
        attn_near = gather_near(attn_input, n_mp)
        lanes = lax.broadcasted_iota(jnp.int32, (1, PAIR), 1)
        half_items = [
            jnp.concatenate(item_blocks[: n_mp // 2]),
            jnp.concatenate(item_blocks[n_mp // 2 :]),
        ]
        picks = [(items[:, None] == lanes).astype(BF16) for items in half_items]
        bars = [
            jnp.where(items[:, None] == lanes, 0.0, EXCLUDED).astype(BF16) for items in half_items
        ]
        bias_wide = jnp.concatenate([input_bias[0], jnp.zeros_like(input_bias[0]), input_bias[1]])
        weight_wide = jnp.concatenate([input_weight[0], input_weight[1], input_weight[2]], 1)

        def project(rows):
            return (dot_nn(rows, weight_wide) + bias_wide).astype(BF16)

        near = project(attn_near)
        far_own, near, grad_low = tie(far_own, near, grad_low)
        attn_far = gather_near(far_own, n_mp)
        grad_far = swap(grad_low, "mp", n_mp, far_bit)
        far = project(attn_far)

        heads_far, logs_far = attend_forward(far, picks[1], [near, far], bars)
        near_count = n_mp // 2

        def cut(rows):
            rows = rows.astype(BF16)
            return [rows[j * own_count : (j + 1) * own_count] for j in range(near_count)]

        sum_far = add_up(scatter_near(cut(dot_nn(heads_far, output_weight)), n_mp)).astype(BF16)
        sum_far, near = tie(sum_far, near)
        arrived = swap(sum_far, "mp", n_mp, far_bit)
        heads_near, logs_near = attend_forward(near, picks[0], [near, far], bars)
        sum_near = scatter_near(cut(dot_nn(heads_near, output_weight)), n_mp)
        grad_near = gather_near(grad_low, n_mp)
        grad_far = gather_near(grad_far, n_mp)
        arrived, grad_near, grad_far = tie(arrived, grad_near, grad_far)
        hidden_res = residual + (add_up(sum_near) + arrived.astype(F32)) + output_bias
        normed_two, inverse_two = normalize(hidden_res)
        mlp_input = (normed_two * second_gain + second_shift).astype(BF16)

        far_own = swap(mlp_input, "mp", n_mp, far_bit)
        mlp_near = gather_near(mlp_input, n_mp)
        act_near, slope_near, back_near = mlp_both(
            mlp_near, grad_near, expand_weight, expand_bias, reduce_weight
        )
        far_own, act_near, slope_near, back_near = tie(far_own, act_near, slope_near, back_near)
        mlp_far = gather_near(far_own, n_mp)
        sum_near = scatter_near(cut(back_near), n_mp)
        act_far, slope_far, back_far = mlp_both(
            mlp_far, grad_far, expand_weight, expand_bias, reduce_weight
        )
        act_far, slope_far, back_far, *sum_near = tie(act_far, slope_far, back_far, *sum_near)
        swapped = dp_bits[1:2] + dp_bits[:1] + dp_bits[2:]
        reduce_sum = DpSum(n_dp, group, dp_bits)
        expand_sum = DpSum(n_dp, group, swapped)
        output_sum = DpSum(n_dp, group, dp_bits)
        input_sum = DpSum(n_dp, group, dp_bits)
        sum_far = add_up(scatter_near(cut(back_far), n_mp)).astype(BF16)
        reduce_sum.open([(act_near, grad_near), (act_far, grad_far)])
        sum_far, slope_near, slope_far, act_far = start_all(
            (sum_far, slope_near, slope_far, act_far), [reduce_sum]
        )
        arrived = swap(sum_far, "mp", n_mp, far_bit)
        expand_sum.open([(mlp_near, slope_near), (mlp_far, slope_far)])
        sum_near[0], act_near, act_far, slope_near, slope_far = start_all(
            (sum_near[0], act_near, act_far, slope_near, slope_far), [expand_sum]
        )
        reduce_sum.keep([(act_near, grad_near), (act_far, grad_far)])
        expand_sum.keep([(mlp_near, slope_near), (mlp_far, slope_far)])
        out_far = scatter_near(cut(dot_nn(act_far, reduce_weight)), n_mp)
        out_near = scatter_near(cut(dot_nn(act_near, reduce_weight)), n_mp)
        held = [reduce_sum.held, expand_sum.held]
        arrived, *held = tie(arrived, *held, *out_far, *out_near)
        reduce_sum.held, expand_sum.held = held[:2]
        out_far, out_near = held[2:4], held[4:]

        normed_grad_two = add_up(sum_near) + arrived.astype(F32)
        grad_out = grad_low.astype(F32)
        residual_grad = grad_out + normalize_back(
            normed_grad_two, normed_two, inverse_two, second_gain
        )
        branch_grad = residual_grad.astype(BF16)
        far_own = swap(branch_grad, "mp", n_mp, far_bit)
        branch_near = gather_near(branch_grad, n_mp)
        head_near = dot_nt(branch_near, output_weight).astype(BF16)
        query_near, key_part, value_part = attend_back(
            near, picks[0], head_near, heads_near, logs_near, [near, far], bars, None, False
        )
        far_own, query_near, normed_grad_two, branch_grad, *out_far = await_all(
            (far_own, query_near, normed_grad_two, branch_grad, *out_far),
            [reduce_sum, expand_sum],
        )
        branch_far = gather_near(far_own, n_mp)
        (branch_far,) = start_all((branch_far,), [reduce_sum, expand_sum])
        branch_pairs = [(heads_near, branch_near), (heads_far, branch_far)]
        output_sum.open(branch_pairs)
        head_far = dot_nt(branch_far, output_weight).astype(BF16)
        (head_far,) = start_all((head_far,), [output_sum])
        query_far, key_grads, value_grads = attend_back(
            far,
            picks[1],
            head_far,
            heads_far,
            logs_far,
            [near, far],
            bars,
            (key_part, value_part),
            True,
        )
        query_far, query_near, branch_far, normed_grad_two, branch_grad, *out_far = await_all(
            (query_far, query_near, branch_far, normed_grad_two, branch_grad, *out_far),
            [reduce_sum, expand_sum],
        )
        qkv_far = jnp.concatenate([query_far, key_grads[1], value_grads[1]], 1)
        sum_far = scatter_near(cut(dot_nt(qkv_far, weight_wide)), n_mp)
        qkv_near = jnp.concatenate([query_near, key_grads[0], value_grads[0]], 1)
        (qkv_near,) = start_all((qkv_near,), [reduce_sum, expand_sum])
        pairs = [(attn_near, qkv_near), (attn_far, qkv_far)]
        input_sum.open(pairs)
        sum_far, qkv_near = start_all((add_up(sum_far).astype(BF16), qkv_near), [input_sum])
        arrived = swap(sum_far, "mp", n_mp, far_bit)
        sum_near = scatter_near(cut(dot_nt(qkv_near, weight_wide)), n_mp)
        input_sum.keep(pairs)
        output_sum.keep([(heads_near, branch_near), (heads_far, branch_far)])
        arrived, input_sum.held, output_sum.held, *sum_near = tie(
            arrived, input_sum.held, output_sum.held, *sum_near
        )
        normed_grad_one = add_up(sum_near) + arrived.astype(F32)
        input_gradient = residual_grad + normalize_back(
            normed_grad_one, normed_one, inverse_one, first_gain
        )
        both = butterfly(
            jnp.stack(
                [
                    jnp.sum(normed_grad_two * normed_two, 0),
                    jnp.sum(normed_grad_two, 0),
                    jnp.sum(branch_grad, 0, dtype=F32),
                    jnp.sum(grad_out, 0),
                    jnp.sum(normed_grad_one * normed_one, 0),
                    jnp.sum(normed_grad_one, 0),
                ]
            ),
            (("mp", n_mp),),
        )
        hidden = expand_bias.shape[0]
        hidden_sums = jnp.sum(slope_near, 0, dtype=F32) + jnp.sum(slope_far, 0, dtype=F32)
        wide_sums = jnp.sum(qkv_near, 0, dtype=F32) + jnp.sum(qkv_far, 0, dtype=F32)
        small = SmallSum(
            n_dp,
            dp_bits,
            jnp.concatenate(
                [
                    both.reshape(-1),
                    wide_sums[:local_width],
                    wide_sums[2 * local_width :],
                    hidden_sums,
                    jnp.full((PAIR,), jnp.sum(lengths).astype(F32)),
                ]
            ),
        )
        sums = [reduce_sum, expand_sum, output_sum, input_sum]
        token, small.send = await_all((input_gradient, small.send), sums)
        token, *out_far = start_all((token, *out_far), sums)
        token, out_far = tie(token, add_up(out_far).astype(BF16))
        out_far = swap(out_far, "mp", n_mp, far_bit)
        (token,) = await_all((token,), sums)
        sums.append(small)
        (token,) = start_all((token,), sums)
        token, out_far = await_all((token, out_far), sums)
        block_output = (
            hidden_res + (add_up(out_near) + out_far.astype(F32)) + reduce_bias
        ).astype(BF16)
        while any(s.busy() for s in sums):
            sums = [s for s in sums if s.busy()]
            (token,) = start_all((token,), sums)
            (token,) = await_all((token,), sums)
        input_gradient = token

        total = small.held
        rows = total[: 6 * width].reshape(6, width)
        rest = total[6 * width :]
        factor = lax.rsqrt(rest[2 * local_width + hidden])
        rows = rows * factor
        input_total = input_sum.held.astype(F32) * factor
        return (
            block_output,
            input_gradient,
            rows[4],
            rows[5],
            jnp.stack(
                [input_total[:, t * local_width : (t + 1) * local_width] for t in range(3)]
            ),
            rest[: 2 * local_width].reshape(2, local_width) * factor,
            output_sum.held.astype(F32) * factor,
            rows[2],
            rows[0],
            rows[1],
            expand_sum.held.astype(F32) * factor,
            rest[2 * local_width : 2 * local_width + hidden] * factor,
            reduce_sum.held.astype(F32) * factor,
            rows[3],
        )
    return per_device


def solution(mesh):
    placed = (
        P(("dp", "mp"), None),
        P(("dp", "mp"), None),
        P("dp"),
        P("dp", None),
        P("dp"),
        P(),
        P(),
        P(None, None, "mp"),
        P(None, "mp"),
        P("mp", None),
        P(),
        P(),
        P(),
        P(None, "mp"),
        P("mp"),
        P("mp", None),
        P(),
    )
    return jax.shard_map(
        layer((mesh.shape["dp"], mesh.shape["mp"])),
        mesh=mesh,
        in_specs=placed,
        out_specs=(
            P(("dp", "mp"), None),
            P(("dp", "mp"), None),
            P(),
            P(),
            P(None, None, "mp"),
            P(None, "mp"),
            P("mp", None),
            P(),
            P(),
            P(),
            P(None, "mp"),
            P("mp"),
            P("mp", None),
            P(),
        ),
        check_vma=False,
    )
```

```python
import functools
import jax
import jax.numpy as jnp
from jax import lax
from jax.experimental import pallas as pl
from jax.experimental.pallas import tpu as pltpu
from jax.sharding import PartitionSpec as P

F32 = jnp.float32
BF16 = jnp.bfloat16
PAIR = 128
HD = 64
EXCLUDED = -1e30
LIGHT = pl.CostEstimate(flops=1024, bytes_accessed=1024, transcendentals=0)


def dot_nn(a, b):
    return lax.dot_general(a, b, (((1,), (0,)), ((), ())), preferred_element_type=F32)


def dot_nt(a, b):
    return lax.dot_general(a, b, (((1,), (1,)), ((), ())), preferred_element_type=F32)


def dot_tn(a, b):
    return lax.dot_general(a, b, (((0,), (0,)), ((), ())), preferred_element_type=F32)


def head_lanes(head):
    lane = lax.broadcasted_iota(jnp.int32, (1, PAIR), 1)
    return (lane >= head * HD) & (lane < (head + 1) * HD)


def attend_kernel(halves, q_ref, pick_ref, *refs):
    k_refs, v_refs, bar_refs = (
        refs[:halves],
        refs[halves : 2 * halves],
        refs[2 * halves : 3 * halves],
    )
    out_ref, log_ref = refs[3 * halves :]
    scaled = q_ref[...] * jnp.asarray(HD**-0.5, BF16)
    pick = pick_ref[...]
    keys = [jnp.concatenate([k[...], b[...]], 1) for k, b in zip(k_refs, bar_refs)]
    rows = []
    for head in range(2):
        own = jnp.where(head_lanes(head), scaled, jnp.zeros_like(scaled))
        probe = jnp.concatenate([own, pick], 1)
        scores = [dot_nt(k, probe) for k in keys]
        top = functools.reduce(
            jnp.maximum, [jnp.max(s, 0, keepdims=True) for s in scores]
        )
        powers = [jnp.exp(s - top) for s in scores]
        total = functools.reduce(
            jnp.add, [jnp.sum(p, 0, keepdims=True) for p in powers]
        )
        summed = functools.reduce(
            jnp.add, [dot_tn(v[...], p.astype(BF16)) for v, p in zip(v_refs, powers)]
        )
        rows.append((summed / total)[head * HD : (head + 1) * HD])
        log_ref[0, head : head + 1, :] = top + jnp.log(total)
    out_ref[...] = jnp.concatenate(rows, 0).T.astype(BF16)


def attend_forward(own, pick, halves, bars, tile=256):
    count = own.shape[0]
    width = own.shape[1] // 3
    pairs = width // PAIR
    tile = min(tile, count)
    key_spec = [pl.BlockSpec((h.shape[0], PAIR), lambda p, i: (0, pairs + p)) for h in halves]
    value_spec = [pl.BlockSpec((h.shape[0], PAIR), lambda p, i: (0, 2 * pairs + p)) for h in halves]
    bar_spec = [pl.BlockSpec((b.shape[0], PAIR), lambda p, i: (0, 0)) for b in bars]
    total_keys = sum(h.shape[0] for h in halves)
    return pl.pallas_call(
        functools.partial(attend_kernel, len(halves)),
        grid=(pairs, count // tile),
        in_specs=[
            pl.BlockSpec((tile, PAIR), lambda p, i: (i, p)),
            pl.BlockSpec((tile, PAIR), lambda p, i: (i, 0)),
            *key_spec,
            *value_spec,
            *bar_spec,
        ],
        out_specs=[
            pl.BlockSpec((tile, PAIR), lambda p, i: (i, p)),
            pl.BlockSpec((1, 8, tile), lambda p, i: (p, 0, i)),
        ],
        out_shape=[
            jax.ShapeDtypeStruct((count, width), BF16),
            jax.ShapeDtypeStruct((pairs, 8, count), F32),
        ],
        cost_estimate=LIGHT,
        compiler_params=pltpu.CompilerParams(vmem_limit_bytes=24 * 2**20),
        name="attend_forward",
    )(own, pick, *halves, *halves, *bars)


def attend_back_kernel(halves, first, last, q_ref, pick_ref, grad_ref, out_ref, log_ref, *refs):
    k_refs, v_refs, bar_refs = (
        refs[:halves],
        refs[halves : 2 * halves],
        refs[2 * halves : 3 * halves],
    )
    rest = refs[3 * halves :]
    if not first:
        k_in, v_in = rest[:halves], rest[halves : 2 * halves]
        rest = rest[2 * halves :]
    q_grad_ref = rest[0]
    k_out, v_out = rest[1 : 1 + halves], rest[1 + halves : 1 + 2 * halves]
    if last:
        k_sum, v_sum = (
            rest[1 + 2 * halves : 1 + 3 * halves],
            rest[1 + 3 * halves : 1 + 4 * halves],
        )
    else:
        k_sum, v_sum = k_out, v_out
    step = pl.program_id(1)

    @pl.when(step == 0)
    def _():
        for n in range(halves):
            if first:
                k_sum[n][...] = jnp.zeros_like(k_sum[n])
                v_sum[n][...] = jnp.zeros_like(v_sum[n])
            else:
                k_sum[n][...] = k_in[n][...]
                v_sum[n][...] = v_in[n][...]

    scaled = q_ref[...] * jnp.asarray(HD**-0.5, BF16)
    grad = grad_ref[...]
    pick = pick_ref[...]
    both = (grad.astype(F32) * out_ref[...].astype(F32)).T
    owns = [jnp.where(head_lanes(h), scaled, jnp.zeros_like(scaled)) for h in range(2)]
    grads = [jnp.where(head_lanes(h), grad, jnp.zeros_like(grad)) for h in range(2)]
    probes = [jnp.concatenate([own, pick], 1) for own in owns]
    centers = [jnp.sum(both[h * HD : (h + 1) * HD], 0, keepdims=True) for h in range(2)]
    stacked_q = jnp.concatenate(owns, 0)
    stacked_g = jnp.concatenate(grads, 0)
    q_parts = [0.0, 0.0]
    for n in range(halves):
        keys = k_refs[n][...]
        values = v_refs[n][...]
        wide = jnp.concatenate([keys, bar_refs[n][...]], 1)
        probs = []
        slopes = []
        for h in range(2):
            prob = jnp.exp(dot_nt(wide, probes[h]) - log_ref[0, h : h + 1, :])
            slope = (prob * (dot_nt(values, grads[h]) - centers[h])).astype(BF16)
            probs.append(prob.astype(BF16))
            slopes.append(slope)
            q_parts[h] = q_parts[h] + dot_tn(keys, slope)
        v_sum[n][...] += dot_nn(jnp.concatenate(probs, 1), stacked_g)
        k_sum[n][...] += dot_nn(jnp.concatenate(slopes, 1), stacked_q)
    rows = [q_parts[h][h * HD : (h + 1) * HD] * (HD**-0.5) for h in range(2)]
    q_grad_ref[...] = jnp.concatenate(rows, 0).T.astype(BF16)

    if last:

        @pl.when(step == pl.num_programs(1) - 1)
        def _():
            for n in range(halves):
                k_out[n][...] = k_sum[n][...].astype(BF16)
                v_out[n][...] = v_sum[n][...].astype(BF16)


def attend_back(own, pick, grad, out, logs, halves, bars, carried, last, tile=256):
    count = own.shape[0]
    width = own.shape[1] // 3
    pairs = width // PAIR
    tile = min(tile, count)
    first = carried is None
    key_spec = [pl.BlockSpec((h.shape[0], PAIR), lambda p, i: (0, pairs + p)) for h in halves]
    value_spec = [pl.BlockSpec((h.shape[0], PAIR), lambda p, i: (0, 2 * pairs + p)) for h in halves]
    bar_spec = [pl.BlockSpec((b.shape[0], PAIR), lambda p, i: (0, 0)) for b in bars]
    sum_spec = [pl.BlockSpec((h.shape[0], PAIR), lambda p, i: (0, p)) for h in halves]
    row_spec = pl.BlockSpec((tile, PAIR), lambda p, i: (i, p))
    sum_type = BF16 if last else F32
    sums = [jax.ShapeDtypeStruct((h.shape[0], width), sum_type) for h in halves]
    total_keys = sum(h.shape[0] for h in halves)
    scratch = []
    if last:
        scratch = [pltpu.VMEM((h.shape[0], PAIR), F32) for h in halves] * 2
    extra = [] if first else list(carried[0]) + list(carried[1])
    parts = len(halves)
    result = pl.pallas_call(
        functools.partial(attend_back_kernel, parts, first, last),
        grid=(pairs, count // tile),
        in_specs=[
            row_spec,
            pl.BlockSpec((tile, PAIR), lambda p, i: (i, 0)),
            row_spec,
            row_spec,
            pl.BlockSpec((1, 8, tile), lambda p, i: (p, 0, i)),
            *key_spec,
            *value_spec,
            *bar_spec,
            *([] if first else sum_spec * 2),
        ],
        out_specs=[row_spec, *sum_spec, *sum_spec],
        out_shape=[jax.ShapeDtypeStruct((count, width), BF16), *sums, *sums],
        scratch_shapes=scratch,
        cost_estimate=LIGHT,
        compiler_params=pltpu.CompilerParams(vmem_limit_bytes=24 * 2**20),
        name="attend_back",
    )(own, pick, grad, out, logs, *halves, *halves, *bars, *extra)
    return result[0], result[1 : 1 + parts], result[1 + parts :]


def mlp_kernel(x_ref, grad_ref, up_ref, bias_ref, down_ref, act_ref, slope_ref, back_ref, *share_ref):
    pre = dot_nn(x_ref[...], up_ref[...]) + bias_ref[...]
    upstream = dot_nt(grad_ref[...], down_ref[...])
    cdf = 0.5 + 0.5 * lax.erf(pre * (0.5**0.5))
    act = (pre * cdf).astype(BF16)
    act_ref[...] = act
    if share_ref:
        share_ref[0][...] = dot_nn(act, down_ref[...]).astype(BF16)
    density = jnp.exp(-0.5 * pre * pre) * 0.3989422804014327
    slope = (upstream * (cdf + pre * density)).astype(BF16)
    slope_ref[...] = slope
    back_ref[...] = dot_nt(slope, up_ref[...]).astype(BF16)


def mlp_both(x, grad, up, bias, down, share, tile=256):
    count, width = x.shape
    hidden = up.shape[1]
    tile = min(tile, count)
    whole = lambda i: (0, 0)
    return pl.pallas_call(
        mlp_kernel,
        grid=(count // tile,),
        in_specs=[
            pl.BlockSpec((tile, width), lambda i: (i, 0)),
            pl.BlockSpec((tile, width), lambda i: (i, 0)),
            pl.BlockSpec((width, hidden), whole, pipeline_mode=pl.Buffered(1)),
            pl.BlockSpec((1, hidden), whole),
            pl.BlockSpec((hidden, width), whole, pipeline_mode=pl.Buffered(1)),
        ],
        out_specs=[
            pl.BlockSpec((tile, hidden), lambda i: (i, 0)),
            pl.BlockSpec((tile, hidden), lambda i: (i, 0)),
            *[pl.BlockSpec((tile, width), lambda i: (i, 0))] * (1 + share),
        ],
        out_shape=[
            jax.ShapeDtypeStruct((count, hidden), BF16),
            jax.ShapeDtypeStruct((count, hidden), BF16),
            *[jax.ShapeDtypeStruct((count, width), BF16)] * (1 + share),
        ],
        cost_estimate=LIGHT,
        compiler_params=pltpu.CompilerParams(vmem_limit_bytes=24 * 2**20),
        name="mlp_both",
    )(x, grad, up, bias[None], down)


EPSILON = 1e-06


def normalize(values):
    center = values - jnp.mean(values, -1, keepdims=True)
    inverse = lax.rsqrt(jnp.mean(center * center, -1, keepdims=True) + EPSILON)
    return (center * inverse, inverse)


def normalize_back(upstream, normed, inverse, gain):
    scaled = upstream * gain
    return inverse * (
        scaled
        - jnp.mean(scaled, -1, keepdims=True)
        - normed * jnp.mean(scaled * normed, -1, keepdims=True)
    )


def position_rows(own_items, item_lengths, level, first_row, width):
    slot_count = item_lengths.shape[0]
    slot_index = lax.broadcasted_iota(jnp.int32, (1, slot_count), 1)
    start_row = jnp.sum(jnp.where(slot_index < own_items[:, None], item_lengths[None, :], 0), 1)
    row_index = first_row + jnp.arange(own_items.shape[0], dtype=jnp.int32)
    valid_rows = (own_items < slot_count).astype(F32)
    level_ratio = jnp.exp2(level.astype(F32) - 2.0)
    places = (row_index - start_row).astype(F32) * level_ratio
    half_width = width // 2
    frequency = jnp.exp(-jnp.log(10000.0) * jnp.arange(half_width, dtype=F32) / half_width)
    angles = places[:, None] * frequency[None, :]
    return (
        jnp.concatenate([jnp.sin(angles), jnp.cos(angles)], 1) * valid_rows[:, None],
        valid_rows,
    )


def bits_of(size):
    bits = []
    step = 1
    while step < size:
        bits.append(step)
        step *= 2
    return bits


def tie(*arrays):
    return lax.optimization_barrier(arrays)


def swap(array, axis, size, bit):
    return lax.ppermute(array, axis, [(i, i ^ bit) for i in range(size)])


def gather_near(own, count):
    blocks = {0: own}
    for bit in reversed(bits_of(count)[:-1]):
        blocks.update(
            {j | bit: swap(rows, "mp", count, bit) for j, rows in list(blocks.items())}
        )
    return jnp.concatenate([blocks[j] for j in range(count // 2)])


def scatter_near(pieces, count):
    held = dict(enumerate(pieces))
    bits = bits_of(count)[:-1]
    for bit in bits:
        arrived = {
            j ^ bit: swap(held[j].astype(BF16), "mp", count, bit) for j in held if j & bit
        }
        if bit == bits[-1]:
            return held[0], arrived[0]
        held = {j: held[j].astype(F32) + arrived[j].astype(F32) for j in arrived}


def add_up(pair):
    return pair[0].astype(F32) + pair[1].astype(F32)


class DpSum:
    def __init__(self, count, index, order):
        self.count, self.index = count, index
        self.order = order
        self.steps = list(order) + list(reversed(order))
        self.at = 0

    def high(self, bit):
        return (self.index & bit) != 0

    def half(self, pairs, other):
        size = pairs[0][0].shape[1] // 2
        top = jnp.where(self.high(self.order[0]) != other, size, 0)
        dots = [
            dot_tn(lax.dynamic_slice_in_dim(left, top, size, 1), right) for left, right in pairs
        ]
        return functools.reduce(jnp.add, dots).astype(BF16)

    def open(self, pairs):
        self.send = self.half(pairs, True)

    def keep(self, pairs):
        self.held = self.half(pairs, False)

    def launch(self):
        self.flying = swap(self.send, "dp", self.count, self.steps[self.at])

    def land(self):
        bit = self.steps[self.at]
        if self.at < len(self.order):
            self.held = (self.held.astype(F32) + self.flying.astype(F32)).astype(BF16)
        else:
            self.held = jnp.where(
                self.high(bit),
                jnp.concatenate([self.flying, self.held]),
                jnp.concatenate([self.held, self.flying]),
            )
        self.at += 1
        if self.at < len(self.order):
            rows, width = self.held.shape
            halves = self.held.reshape(2, rows // 2, width)
            place = self.high(self.steps[self.at]).astype(jnp.int32)
            self.send = lax.dynamic_index_in_dim(halves, 1 - place, 0, False)
            self.held = lax.dynamic_index_in_dim(halves, place, 0, False)
        else:
            self.send = self.held

    def busy(self):
        return self.at < len(self.steps)


class SmallSum:
    def __init__(self, count, order, values):
        self.count, self.steps, self.at = count, list(order), 0
        self.send = self.held = values

    def launch(self):
        self.held = self.send
        self.flying = swap(self.send, "dp", self.count, self.steps[self.at])

    def land(self):
        self.send = self.held = self.held + self.flying
        self.at += 1

    def busy(self):
        return self.at < len(self.steps)


def await_all(chain, sums):
    tied = tie(*chain, *[s.flying for s in sums])
    for s, value in zip(sums, tied[len(chain) :]):
        s.flying = value
        s.land()
    return tied[: len(chain)]


def start_all(chain, sums):
    sums = [s for s in sums if s.busy()]
    tied = tie(*chain, *[s.send for s in sums])
    for s, value in zip(sums, tied[len(chain) :]):
        s.send = value
        s.launch()
    return tied[: len(chain)]


def butterfly(values, sizes):
    for axis, size in sizes:
        for bit in bits_of(size):
            values = values + swap(values, axis, size, bit)
    return values


def layer(sizes):
    n_dp, n_mp = sizes
    far_bit = n_mp // 2
    dp_bits = bits_of(n_dp)

    def per_device(
        tokens,
        cotangent,
        segments,
        lengths,
        scale_levels,
        first_gain,
        first_shift,
        input_weight,
        input_bias,
        output_weight,
        output_bias,
        second_gain,
        second_shift,
        expand_weight,
        expand_bias,
        reduce_weight,
        reduce_bias,
    ):
        me = lax.axis_index("mp")
        group = lax.axis_index("dp")
        own_count, width = tokens.shape
        local_width = input_weight.shape[2]
        half_count = own_count * n_mp // 2
        item_blocks = [
            lax.dynamic_slice_in_dim(segments, (me ^ j) * own_count, own_count)
            for j in range(n_mp)
        ]
        positions, valid_rows = position_rows(
            item_blocks[0], lengths[0], scale_levels[0], me * own_count, width
        )
        residual = tokens.astype(F32) + positions
        normed_one, inverse_one = normalize(residual)
        attn_input = (normed_one * first_gain + first_shift).astype(BF16)
        grad_low = (cotangent.astype(F32) * valid_rows[:, None]).astype(BF16)

        far_own = swap(attn_input, "mp", n_mp, far_bit)
        attn_near = gather_near(attn_input, n_mp)
        lanes = lax.broadcasted_iota(jnp.int32, (1, PAIR), 1)
        half_items = [
            jnp.concatenate(item_blocks[: n_mp // 2]),
            jnp.concatenate(item_blocks[n_mp // 2 :]),
        ]
        picks = [(items[:, None] == lanes).astype(BF16) for items in half_items]
        bars = [
            jnp.where(items[:, None] == lanes, 0.0, EXCLUDED).astype(BF16) for items in half_items
        ]
        bias_wide = jnp.concatenate([input_bias[0], jnp.zeros_like(input_bias[0]), input_bias[1]])
        weight_wide = jnp.concatenate([input_weight[0], input_weight[1], input_weight[2]], 1)

        def project(rows):
            return (dot_nn(rows, weight_wide) + bias_wide).astype(BF16)

        near = project(attn_near)
        far_own, near, grad_low = tie(far_own, near, grad_low)
        attn_far = gather_near(far_own, n_mp)
        grad_far = swap(grad_low, "mp", n_mp, far_bit)
        far = project(attn_far)

        heads_far, logs_far = attend_forward(far, picks[1], [near, far], bars)
        near_count = n_mp // 2

        def cut(rows):
            rows = rows.astype(BF16)
            return [rows[j * own_count : (j + 1) * own_count] for j in range(near_count)]

        sum_far = add_up(scatter_near(cut(dot_nn(heads_far, output_weight)), n_mp)).astype(BF16)
        sum_far, near = tie(sum_far, near)
        arrived = swap(sum_far, "mp", n_mp, far_bit)
        heads_near, logs_near = attend_forward(near, picks[0], [near, far], bars)
        sum_near = scatter_near(cut(dot_nn(heads_near, output_weight)), n_mp)
        grad_near = gather_near(grad_low, n_mp)
        grad_far = gather_near(grad_far, n_mp)
        arrived, grad_near, grad_far = tie(arrived, grad_near, grad_far)
        hidden_res = residual + (add_up(sum_near) + arrived.astype(F32)) + output_bias
        normed_two, inverse_two = normalize(hidden_res)
        mlp_input = (normed_two * second_gain + second_shift).astype(BF16)

        far_own = swap(mlp_input, "mp", n_mp, far_bit)
        mlp_near = gather_near(mlp_input, n_mp)
        act_near, slope_near, back_near, share_near = mlp_both(
            mlp_near, grad_near, expand_weight, expand_bias, reduce_weight, True
        )
        far_own, act_near, slope_near, back_near, share_near = tie(
            far_own, act_near, slope_near, back_near, share_near
        )
        mlp_far = gather_near(far_own, n_mp)
        sum_near = scatter_near(cut(back_near), n_mp)
        act_far, slope_far, back_far, share_far = mlp_both(
            mlp_far, grad_far, expand_weight, expand_bias, reduce_weight, True
        )
        act_far, slope_far, back_far, *sum_near = tie(act_far, slope_far, back_far, *sum_near)
        swapped = dp_bits[1:2] + dp_bits[:1] + dp_bits[2:]
        reduce_sum = DpSum(n_dp, group, dp_bits)
        expand_sum = DpSum(n_dp, group, swapped)
        output_sum = DpSum(n_dp, group, dp_bits)
        input_sum = DpSum(n_dp, group, dp_bits)
        sum_far = add_up(scatter_near(cut(back_far), n_mp)).astype(BF16)
        reduce_sum.open([(act_near, grad_near), (act_far, grad_far)])
        sum_far, slope_near, slope_far, act_far = start_all(
            (sum_far, slope_near, slope_far, act_far), [reduce_sum]
        )
        arrived = swap(sum_far, "mp", n_mp, far_bit)
        expand_sum.open([(mlp_near, slope_near), (mlp_far, slope_far)])
        sum_near[0], act_near, act_far, slope_near, slope_far = start_all(
            (sum_near[0], act_near, act_far, slope_near, slope_far), [expand_sum]
        )
        reduce_sum.keep([(act_near, grad_near), (act_far, grad_far)])
        expand_sum.keep([(mlp_near, slope_near), (mlp_far, slope_far)])
        out_far = scatter_near(cut(share_far), n_mp)
        out_near = scatter_near(cut(share_near), n_mp)
        held = [reduce_sum.held, expand_sum.held]
        arrived, *held = tie(arrived, *held, *out_far, *out_near)
        reduce_sum.held, expand_sum.held = held[:2]
        out_far, out_near = held[2:4], held[4:]

        normed_grad_two = add_up(sum_near) + arrived.astype(F32)
        grad_out = grad_low.astype(F32)
        residual_grad = grad_out + normalize_back(
            normed_grad_two, normed_two, inverse_two, second_gain
        )
        branch_grad = residual_grad.astype(BF16)
        far_own = swap(branch_grad, "mp", n_mp, far_bit)
        branch_near = gather_near(branch_grad, n_mp)
        head_near = dot_nt(branch_near, output_weight).astype(BF16)
        query_near, key_part, value_part = attend_back(
            near, picks[0], head_near, heads_near, logs_near, [near, far], bars, None, False
        )
        far_own, query_near, normed_grad_two, branch_grad, *out_far = await_all(
            (far_own, query_near, normed_grad_two, branch_grad, *out_far),
            [reduce_sum, expand_sum],
        )
        branch_far = gather_near(far_own, n_mp)
        (branch_far,) = start_all((branch_far,), [reduce_sum, expand_sum])
        branch_pairs = [(heads_near, branch_near), (heads_far, branch_far)]
        output_sum.open(branch_pairs)
        head_far = dot_nt(branch_far, output_weight).astype(BF16)
        (head_far,) = start_all((head_far,), [output_sum])
        query_far, key_grads, value_grads = attend_back(
            far,
            picks[1],
            head_far,
            heads_far,
            logs_far,
            [near, far],
            bars,
            (key_part, value_part),
            True,
        )
        tied = (query_near, branch_far, normed_grad_two, branch_grad, grad_low)
        tied = (query_far, *tied, slope_near, slope_far, *out_far)
        tied = await_all(tied, [reduce_sum, expand_sum])
        query_far, query_near, branch_far, normed_grad_two, branch_grad, grad_low = tied[:6]
        slope_near, slope_far, *out_far = tied[6:]
        qkv_far = jnp.concatenate([query_far, key_grads[1], value_grads[1]], 1)
        sum_far = scatter_near(cut(dot_nt(qkv_far, weight_wide)), n_mp)
        qkv_near = jnp.concatenate([query_near, key_grads[0], value_grads[0]], 1)
        (qkv_near,) = start_all((qkv_near,), [reduce_sum, expand_sum])
        pairs = [(attn_near, qkv_near), (attn_far, qkv_far)]
        input_sum.open(pairs)
        sum_far, qkv_near = start_all((add_up(sum_far).astype(BF16), qkv_near), [input_sum])
        arrived = swap(sum_far, "mp", n_mp, far_bit)
        sum_near = scatter_near(cut(dot_nt(qkv_near, weight_wide)), n_mp)
        input_sum.keep(pairs)
        output_sum.keep([(heads_near, branch_near), (heads_far, branch_far)])
        arrived, input_sum.held, output_sum.held, *sum_near = tie(
            arrived, input_sum.held, output_sum.held, *sum_near
        )
        normed_grad_one = add_up(sum_near) + arrived.astype(F32)
        input_gradient = residual_grad + normalize_back(
            normed_grad_one, normed_one, inverse_one, first_gain
        )
        both = butterfly(
            jnp.stack(
                [
                    jnp.sum(normed_grad_two * normed_two, 0),
                    jnp.sum(normed_grad_two, 0),
                    jnp.sum(branch_grad, 0, dtype=F32),
                    jnp.sum(grad_low, 0, dtype=F32),
                    jnp.sum(normed_grad_one * normed_one, 0),
                    jnp.sum(normed_grad_one, 0),
                ]
            ),
            (("mp", n_mp),),
        )
        hidden = expand_bias.shape[0]
        hidden_sums = jnp.sum(slope_near, 0, dtype=F32) + jnp.sum(slope_far, 0, dtype=F32)
        wide_sums = jnp.sum(qkv_near, 0, dtype=F32) + jnp.sum(qkv_far, 0, dtype=F32)
        small = SmallSum(
            n_dp,
            dp_bits,
            jnp.concatenate(
                [
                    both.reshape(-1),
                    wide_sums[:local_width],
                    wide_sums[2 * local_width :],
                    hidden_sums,
                    jnp.full((PAIR,), jnp.sum(lengths).astype(F32)),
                ]
            ),
        )
        sums = [reduce_sum, expand_sum, input_sum, output_sum]
        token, small.send = await_all((input_gradient, small.send), sums)
        token, *out_far = start_all((token, *out_far), sums[:2])
        token, *out_far = start_all((token, *out_far), sums[2:])
        token, out_far = tie(token, add_up(out_far).astype(BF16))
        out_far = swap(out_far, "mp", n_mp, far_bit)
        quick = [input_sum, output_sum, small]
        slow = [reduce_sum, expand_sum]
        waiting = {"f": quick, "s": slow, "r": slow, "e": [], "R": slow[:1], "E": slow[1:]}
        sending = {"f": quick, "s": slow, "r": slow[:1], "e": slow[1:], "R": [], "E": []}
        flying = list(sums)
        totals = {}
        turns = "fsfsffsf" if len(dp_bits) == 3 else "fs" * 2 * len(dp_bits)
        for n, turn in enumerate(turns):
            if n == 4:
                block_output = (
                    hidden_res + (add_up(out_near) + out_far.astype(F32)) + reduce_bias
                ).astype(BF16)
                token, block_output = tie(token, block_output)
            landing = [s for s in waiting[turn] if s in flying]
            token, out_far = await_all((token, out_far), landing)
            flying = [s for s in flying if s not in landing]
            leaving = [s for s in sending[turn] if s.busy() and s not in flying]
            token, out_far = start_all((token, out_far), leaving)
            flying += leaving
            for s in slow:
                if not (s.busy() or small.busy() or s in totals):
                    factor = lax.rsqrt(small.held[-1])
                    token, totals[s] = tie(token, s.held.astype(F32) * factor)
        if any(s.busy() for s in sums) or flying:
            raise ValueError("unfinished sums")
        input_gradient = token

        total = small.held
        rows = total[: 6 * width].reshape(6, width)
        rest = total[6 * width :]
        factor = lax.rsqrt(rest[2 * local_width + hidden])
        rows = rows * factor
        input_total = input_sum.held.astype(F32) * factor
        return (
            block_output,
            input_gradient,
            rows[4],
            rows[5],
            jnp.stack(
                [input_total[:, t * local_width : (t + 1) * local_width] for t in range(3)]
            ),
            rest[: 2 * local_width].reshape(2, local_width) * factor,
            output_sum.held.astype(F32) * factor,
            rows[2],
            rows[0],
            rows[1],
            totals[expand_sum],
            rest[2 * local_width : 2 * local_width + hidden] * factor,
            totals[reduce_sum],
            rows[3],
        )
    return per_device


def solution(mesh):
    placed = (
        P(("dp", "mp"), None),
        P(("dp", "mp"), None),
        P("dp"),
        P("dp", None),
        P("dp"),
        P(),
        P(),
        P(None, None, "mp"),
        P(None, "mp"),
        P("mp", None),
        P(),
        P(),
        P(),
        P(None, "mp"),
        P("mp"),
        P("mp", None),
        P(),
    )
    return jax.shard_map(
        layer((mesh.shape["dp"], mesh.shape["mp"])),
        mesh=mesh,
        in_specs=placed,
        out_specs=(
            P(("dp", "mp"), None),
            P(("dp", "mp"), None),
            P(),
            P(),
            P(None, None, "mp"),
            P(None, "mp"),
            P("mp", None),
            P(),
            P(),
            P(),
            P(None, "mp"),
            P("mp"),
            P("mp", None),
            P(),
        ),
        check_vma=False,
    )
```

```python
import functools
import jax
import jax.numpy as jnp
from jax import lax
from jax.experimental import pallas as pl
from jax.experimental.pallas import tpu as pltpu
from jax.sharding import PartitionSpec as P

F32 = jnp.float32
BF16 = jnp.bfloat16
PAIR = 128
HD = 64
EXCLUDED = -1e30
LIGHT = pl.CostEstimate(flops=1024, bytes_accessed=1024, transcendentals=0)


def dot_nn(a, b):
    return lax.dot_general(a, b, (((1,), (0,)), ((), ())), preferred_element_type=F32)


def dot_nt(a, b):
    return lax.dot_general(a, b, (((1,), (1,)), ((), ())), preferred_element_type=F32)


def dot_tn(a, b):
    return lax.dot_general(a, b, (((0,), (0,)), ((), ())), preferred_element_type=F32)


def head_lanes(head):
    lane = lax.broadcasted_iota(jnp.int32, (1, PAIR), 1)
    return (lane >= head * HD) & (lane < (head + 1) * HD)


def attend_kernel(halves, q_ref, pick_ref, *refs):
    k_refs, v_refs, bar_refs = (
        refs[:halves],
        refs[halves : 2 * halves],
        refs[2 * halves : 3 * halves],
    )
    out_ref, log_ref = refs[3 * halves :]
    scaled = q_ref[...] * jnp.asarray(HD**-0.5, BF16)
    pick = pick_ref[...]
    keys = [jnp.concatenate([k[...], b[...]], 1) for k, b in zip(k_refs, bar_refs)]
    rows = []
    for head in range(2):
        own = jnp.where(head_lanes(head), scaled, jnp.zeros_like(scaled))
        probe = jnp.concatenate([own, pick], 1)
        scores = [dot_nt(k, probe) for k in keys]
        top = functools.reduce(
            jnp.maximum, [jnp.max(s, 0, keepdims=True) for s in scores]
        )
        powers = [jnp.exp(s - top) for s in scores]
        total = functools.reduce(
            jnp.add, [jnp.sum(p, 0, keepdims=True) for p in powers]
        )
        summed = functools.reduce(
            jnp.add, [dot_tn(v[...], p.astype(BF16)) for v, p in zip(v_refs, powers)]
        )
        rows.append((summed / total)[head * HD : (head + 1) * HD])
        log_ref[0, head : head + 1, :] = top + jnp.log(total)
    out_ref[...] = jnp.concatenate(rows, 0).T.astype(BF16)


def attend_forward(own, pick, halves, bars, tile=256):
    count = own.shape[0]
    width = own.shape[1] // 3
    pairs = width // PAIR
    tile = min(tile, count)
    key_spec = [pl.BlockSpec((h.shape[0], PAIR), lambda p, i: (0, pairs + p)) for h in halves]
    value_spec = [pl.BlockSpec((h.shape[0], PAIR), lambda p, i: (0, 2 * pairs + p)) for h in halves]
    bar_spec = [pl.BlockSpec((b.shape[0], PAIR), lambda p, i: (0, 0)) for b in bars]
    total_keys = sum(h.shape[0] for h in halves)
    return pl.pallas_call(
        functools.partial(attend_kernel, len(halves)),
        grid=(pairs, count // tile),
        in_specs=[
            pl.BlockSpec((tile, PAIR), lambda p, i: (i, p)),
            pl.BlockSpec((tile, PAIR), lambda p, i: (i, 0)),
            *key_spec,
            *value_spec,
            *bar_spec,
        ],
        out_specs=[
            pl.BlockSpec((tile, PAIR), lambda p, i: (i, p)),
            pl.BlockSpec((1, 8, tile), lambda p, i: (p, 0, i)),
        ],
        out_shape=[
            jax.ShapeDtypeStruct((count, width), BF16),
            jax.ShapeDtypeStruct((pairs, 8, count), F32),
        ],
        cost_estimate=LIGHT,
        compiler_params=pltpu.CompilerParams(vmem_limit_bytes=24 * 2**20),
        name="attend_forward",
    )(own, pick, *halves, *halves, *bars)


def attend_back_kernel(halves, first, last, q_ref, pick_ref, grad_ref, out_ref, log_ref, *refs):
    k_refs, v_refs, bar_refs = (
        refs[:halves],
        refs[halves : 2 * halves],
        refs[2 * halves : 3 * halves],
    )
    rest = refs[3 * halves :]
    if not first:
        k_in, v_in = rest[:halves], rest[halves : 2 * halves]
        rest = rest[2 * halves :]
    q_grad_ref = rest[0]
    k_out, v_out = rest[1 : 1 + halves], rest[1 + halves : 1 + 2 * halves]
    if last:
        k_sum, v_sum = (
            rest[1 + 2 * halves : 1 + 3 * halves],
            rest[1 + 3 * halves : 1 + 4 * halves],
        )
    else:
        k_sum, v_sum = k_out, v_out
    step = pl.program_id(1)

    @pl.when(step == 0)
    def _():
        for n in range(halves):
            if first:
                k_sum[n][...] = jnp.zeros_like(k_sum[n])
                v_sum[n][...] = jnp.zeros_like(v_sum[n])
            else:
                k_sum[n][...] = k_in[n][...]
                v_sum[n][...] = v_in[n][...]

    scaled = q_ref[...] * jnp.asarray(HD**-0.5, BF16)
    grad = grad_ref[...]
    pick = pick_ref[...]
    both = (grad.astype(F32) * out_ref[...].astype(F32)).T
    owns = [jnp.where(head_lanes(h), scaled, jnp.zeros_like(scaled)) for h in range(2)]
    grads = [jnp.where(head_lanes(h), grad, jnp.zeros_like(grad)) for h in range(2)]
    probes = [jnp.concatenate([own, pick], 1) for own in owns]
    centers = [jnp.sum(both[h * HD : (h + 1) * HD], 0, keepdims=True) for h in range(2)]
    stacked_q = jnp.concatenate(owns, 0)
    stacked_g = jnp.concatenate(grads, 0)
    q_parts = [0.0, 0.0]
    for n in range(halves):
        keys = k_refs[n][...]
        values = v_refs[n][...]
        wide = jnp.concatenate([keys, bar_refs[n][...]], 1)
        probs = []
        slopes = []
        for h in range(2):
            prob = jnp.exp(dot_nt(wide, probes[h]) - log_ref[0, h : h + 1, :])
            slope = (prob * (dot_nt(values, grads[h]) - centers[h])).astype(BF16)
            probs.append(prob.astype(BF16))
            slopes.append(slope)
            q_parts[h] = q_parts[h] + dot_tn(keys, slope)
        v_sum[n][...] += dot_nn(jnp.concatenate(probs, 1), stacked_g)
        k_sum[n][...] += dot_nn(jnp.concatenate(slopes, 1), stacked_q)
    rows = [q_parts[h][h * HD : (h + 1) * HD] * (HD**-0.5) for h in range(2)]
    q_grad_ref[...] = jnp.concatenate(rows, 0).T.astype(BF16)

    if last:

        @pl.when(step == pl.num_programs(1) - 1)
        def _():
            for n in range(halves):
                k_out[n][...] = k_sum[n][...].astype(BF16)
                v_out[n][...] = v_sum[n][...].astype(BF16)


def attend_back(own, pick, grad, out, logs, halves, bars, carried, last, tile=256):
    count = own.shape[0]
    width = own.shape[1] // 3
    pairs = width // PAIR
    tile = min(tile, count)
    first = carried is None
    key_spec = [pl.BlockSpec((h.shape[0], PAIR), lambda p, i: (0, pairs + p)) for h in halves]
    value_spec = [pl.BlockSpec((h.shape[0], PAIR), lambda p, i: (0, 2 * pairs + p)) for h in halves]
    bar_spec = [pl.BlockSpec((b.shape[0], PAIR), lambda p, i: (0, 0)) for b in bars]
    sum_spec = [pl.BlockSpec((h.shape[0], PAIR), lambda p, i: (0, p)) for h in halves]
    row_spec = pl.BlockSpec((tile, PAIR), lambda p, i: (i, p))
    sum_type = BF16 if last else F32
    sums = [jax.ShapeDtypeStruct((h.shape[0], width), sum_type) for h in halves]
    total_keys = sum(h.shape[0] for h in halves)
    scratch = []
    if last:
        scratch = [pltpu.VMEM((h.shape[0], PAIR), F32) for h in halves] * 2
    extra = [] if first else list(carried[0]) + list(carried[1])
    parts = len(halves)
    result = pl.pallas_call(
        functools.partial(attend_back_kernel, parts, first, last),
        grid=(pairs, count // tile),
        in_specs=[
            row_spec,
            pl.BlockSpec((tile, PAIR), lambda p, i: (i, 0)),
            row_spec,
            row_spec,
            pl.BlockSpec((1, 8, tile), lambda p, i: (p, 0, i)),
            *key_spec,
            *value_spec,
            *bar_spec,
            *([] if first else sum_spec * 2),
        ],
        out_specs=[row_spec, *sum_spec, *sum_spec],
        out_shape=[jax.ShapeDtypeStruct((count, width), BF16), *sums, *sums],
        scratch_shapes=scratch,
        cost_estimate=LIGHT,
        compiler_params=pltpu.CompilerParams(vmem_limit_bytes=24 * 2**20),
        name="attend_back",
    )(own, pick, grad, out, logs, *halves, *halves, *bars, *extra)
    return result[0], result[1 : 1 + parts], result[1 + parts :]


def mlp_kernel(per, x_ref, grad_ref, up_ref, bias_ref, down_ref, act_ref, slope_ref, *piece_refs):
    pre = dot_nn(x_ref[...], up_ref[...]) + bias_ref[...]
    upstream = dot_nt(grad_ref[...], down_ref[...])
    cdf = 0.5 + 0.5 * lax.erf(pre * (0.5**0.5))
    act = (pre * cdf).astype(BF16)
    act_ref[...] = act
    share = dot_nn(act, down_ref[...]).astype(BF16)
    density = jnp.exp(-0.5 * pre * pre) * 0.3989422804014327
    slope = (upstream * (cdf + pre * density)).astype(BF16)
    slope_ref[...] = slope
    back = dot_nt(slope, up_ref[...]).astype(BF16)
    step = pl.program_id(0)
    tile = x_ref.shape[0]
    pieces = len(piece_refs) // 2
    for j in range(pieces):

        @pl.when(step // per == j)
        def _():
            rows = pl.ds(pl.multiple_of((step % per) * tile, tile), tile)
            piece_refs[j][rows, :] = back
            piece_refs[pieces + j][rows, :] = share


def mlp_both(x, grad, up, bias, down, pieces, tile=256):
    count, width = x.shape
    hidden = up.shape[1]
    size = count // pieces
    tile = min(tile, size)
    whole = lambda i: (0, 0)
    return pl.pallas_call(
        functools.partial(mlp_kernel, size // tile),
        grid=(count // tile,),
        in_specs=[
            pl.BlockSpec((tile, width), lambda i: (i, 0)),
            pl.BlockSpec((tile, width), lambda i: (i, 0)),
            pl.BlockSpec((width, hidden), whole, pipeline_mode=pl.Buffered(1)),
            pl.BlockSpec((1, hidden), whole),
            pl.BlockSpec((hidden, width), whole, pipeline_mode=pl.Buffered(1)),
        ],
        out_specs=[
            pl.BlockSpec((tile, hidden), lambda i: (i, 0)),
            pl.BlockSpec((tile, hidden), lambda i: (i, 0)),
            *[pl.BlockSpec((size, width), whole)] * (2 * pieces),
        ],
        out_shape=[
            jax.ShapeDtypeStruct((count, hidden), BF16),
            jax.ShapeDtypeStruct((count, hidden), BF16),
            *[jax.ShapeDtypeStruct((size, width), BF16)] * (2 * pieces),
        ],
        cost_estimate=LIGHT,
        compiler_params=pltpu.CompilerParams(vmem_limit_bytes=24 * 2**20),
        name="mlp_both",
    )(x, grad, up, bias[None], down)


EPSILON = 1e-06


def normalize(values):
    center = values - jnp.mean(values, -1, keepdims=True)
    inverse = lax.rsqrt(jnp.mean(center * center, -1, keepdims=True) + EPSILON)
    return (center * inverse, inverse)


def normalize_back(upstream, normed, inverse, gain):
    scaled = upstream * gain
    return inverse * (
        scaled
        - jnp.mean(scaled, -1, keepdims=True)
        - normed * jnp.mean(scaled * normed, -1, keepdims=True)
    )


def position_rows(own_items, item_lengths, level, first_row, width):
    slot_count = item_lengths.shape[0]
    slot_index = lax.broadcasted_iota(jnp.int32, (1, slot_count), 1)
    start_row = jnp.sum(jnp.where(slot_index < own_items[:, None], item_lengths[None, :], 0), 1)
    row_index = first_row + jnp.arange(own_items.shape[0], dtype=jnp.int32)
    valid_rows = (own_items < slot_count).astype(F32)
    level_ratio = jnp.exp2(level.astype(F32) - 2.0)
    places = (row_index - start_row).astype(F32) * level_ratio
    half_width = width // 2
    frequency = jnp.exp(-jnp.log(10000.0) * jnp.arange(half_width, dtype=F32) / half_width)
    angles = places[:, None] * frequency[None, :]
    return (
        jnp.concatenate([jnp.sin(angles), jnp.cos(angles)], 1) * valid_rows[:, None],
        valid_rows,
    )


def bits_of(size):
    bits = []
    step = 1
    while step < size:
        bits.append(step)
        step *= 2
    return bits


def tie(*arrays):
    return lax.optimization_barrier(arrays)


def swap(array, axis, size, bit):
    return lax.ppermute(array, axis, [(i, i ^ bit) for i in range(size)])


def gather_near(own, count):
    blocks = {0: own}
    for bit in reversed(bits_of(count)[:-1]):
        blocks.update(
            {j | bit: swap(rows, "mp", count, bit) for j, rows in list(blocks.items())}
        )
    return jnp.concatenate([blocks[j] for j in range(count // 2)])


def scatter_near(pieces, count):
    held = dict(enumerate(pieces))
    bits = bits_of(count)[:-1]
    for bit in bits:
        arrived = {
            j ^ bit: swap(held[j].astype(BF16), "mp", count, bit) for j in held if j & bit
        }
        if bit == bits[-1]:
            return held[0], arrived[0]
        held = {j: held[j].astype(F32) + arrived[j].astype(F32) for j in arrived}


def add_up(pair):
    return pair[0].astype(F32) + pair[1].astype(F32)


class DpSum:
    def __init__(self, count, index, order):
        self.count, self.index = count, index
        self.order = order
        self.steps = list(order) + list(reversed(order))
        self.at = 0

    def high(self, bit):
        return (self.index & bit) != 0

    def half(self, pairs, other):
        size = pairs[0][0].shape[1] // 2
        top = jnp.where(self.high(self.order[0]) != other, size, 0)
        dots = [
            dot_tn(lax.dynamic_slice_in_dim(left, top, size, 1), right) for left, right in pairs
        ]
        return functools.reduce(jnp.add, dots).astype(BF16)

    def open(self, pairs):
        self.send = self.half(pairs, True)

    def keep(self, pairs):
        self.held = self.half(pairs, False)

    def launch(self):
        self.flying = swap(self.send, "dp", self.count, self.steps[self.at])

    def land(self):
        bit = self.steps[self.at]
        if self.at < len(self.order):
            self.held = (self.held.astype(F32) + self.flying.astype(F32)).astype(BF16)
        else:
            self.held = jnp.where(
                self.high(bit),
                jnp.concatenate([self.flying, self.held]),
                jnp.concatenate([self.held, self.flying]),
            )
        self.at += 1
        if self.at < len(self.order):
            rows, width = self.held.shape
            halves = self.held.reshape(2, rows // 2, width)
            place = self.high(self.steps[self.at]).astype(jnp.int32)
            self.send = lax.dynamic_index_in_dim(halves, 1 - place, 0, False)
            self.held = lax.dynamic_index_in_dim(halves, place, 0, False)
        else:
            self.send = self.held

    def busy(self):
        return self.at < len(self.steps)


class SmallSum:
    def __init__(self, count, order, values):
        self.count, self.steps, self.at = count, list(order), 0
        self.send = self.held = values

    def launch(self):
        self.held = self.send
        self.flying = swap(self.send, "dp", self.count, self.steps[self.at])

    def land(self):
        self.send = self.held = self.held + self.flying
        self.at += 1

    def busy(self):
        return self.at < len(self.steps)


def await_all(chain, sums):
    tied = tie(*chain, *[s.flying for s in sums])
    for s, value in zip(sums, tied[len(chain) :]):
        s.flying = value
        s.land()
    return tied[: len(chain)]


def start_all(chain, sums):
    sums = [s for s in sums if s.busy()]
    tied = tie(*chain, *[s.send for s in sums])
    for s, value in zip(sums, tied[len(chain) :]):
        s.send = value
        s.launch()
    return tied[: len(chain)]


def butterfly(values, sizes):
    for axis, size in sizes:
        for bit in bits_of(size):
            values = values + swap(values, axis, size, bit)
    return values


def layer(sizes):
    n_dp, n_mp = sizes
    far_bit = n_mp // 2
    dp_bits = bits_of(n_dp)

    def per_device(
        tokens,
        cotangent,
        segments,
        lengths,
        scale_levels,
        first_gain,
        first_shift,
        input_weight,
        input_bias,
        output_weight,
        output_bias,
        second_gain,
        second_shift,
        expand_weight,
        expand_bias,
        reduce_weight,
        reduce_bias,
    ):
        me = lax.axis_index("mp")
        group = lax.axis_index("dp")
        own_count, width = tokens.shape
        local_width = input_weight.shape[2]
        half_count = own_count * n_mp // 2
        item_blocks = [
            lax.dynamic_slice_in_dim(segments, (me ^ j) * own_count, own_count)
            for j in range(n_mp)
        ]
        positions, valid_rows = position_rows(
            item_blocks[0], lengths[0], scale_levels[0], me * own_count, width
        )
        residual = tokens.astype(F32) + positions
        normed_one, inverse_one = normalize(residual)
        attn_input = (normed_one * first_gain + first_shift).astype(BF16)
        grad_low = (cotangent.astype(F32) * valid_rows[:, None]).astype(BF16)

        far_own = swap(attn_input, "mp", n_mp, far_bit)
        attn_near = gather_near(attn_input, n_mp)
        lanes = lax.broadcasted_iota(jnp.int32, (1, PAIR), 1)
        half_items = [
            jnp.concatenate(item_blocks[: n_mp // 2]),
            jnp.concatenate(item_blocks[n_mp // 2 :]),
        ]
        picks = [(items[:, None] == lanes).astype(BF16) for items in half_items]
        bars = [
            jnp.where(items[:, None] == lanes, 0.0, EXCLUDED).astype(BF16) for items in half_items
        ]
        bias_wide = jnp.concatenate([input_bias[0], jnp.zeros_like(input_bias[0]), input_bias[1]])
        weight_wide = jnp.concatenate([input_weight[0], input_weight[1], input_weight[2]], 1)

        def project(rows):
            return (dot_nn(rows, weight_wide) + bias_wide).astype(BF16)

        near = project(attn_near)
        far_own, near, grad_low = tie(far_own, near, grad_low)
        attn_far = gather_near(far_own, n_mp)
        grad_far = swap(grad_low, "mp", n_mp, far_bit)
        far = project(attn_far)

        heads_far, logs_far = attend_forward(far, picks[1], [near, far], bars)
        near_count = n_mp // 2

        def cut(rows):
            rows = rows.astype(BF16)
            return [rows[j * own_count : (j + 1) * own_count] for j in range(near_count)]

        sum_far = add_up(scatter_near(cut(dot_nn(heads_far, output_weight)), n_mp)).astype(BF16)
        sum_far, near = tie(sum_far, near)
        arrived = swap(sum_far, "mp", n_mp, far_bit)
        heads_near, logs_near = attend_forward(near, picks[0], [near, far], bars)
        sum_near = scatter_near(cut(dot_nn(heads_near, output_weight)), n_mp)
        grad_near = gather_near(grad_low, n_mp)
        grad_far = gather_near(grad_far, n_mp)
        arrived, grad_near, grad_far = tie(arrived, grad_near, grad_far)
        hidden_res = residual + (add_up(sum_near) + arrived.astype(F32)) + output_bias
        normed_two, inverse_two = normalize(hidden_res)
        mlp_input = (normed_two * second_gain + second_shift).astype(BF16)

        far_own = swap(mlp_input, "mp", n_mp, far_bit)
        mlp_near = gather_near(mlp_input, n_mp)
        act_near, slope_near, *pieces_near = mlp_both(
            mlp_near, grad_near, expand_weight, expand_bias, reduce_weight, near_count
        )
        far_own, act_near, slope_near, *pieces_near = tie(
            far_own, act_near, slope_near, *pieces_near
        )
        mlp_far = gather_near(far_own, n_mp)
        sum_near = scatter_near(pieces_near[:near_count], n_mp)
        act_far, slope_far, *pieces_far = mlp_both(
            mlp_far, grad_far, expand_weight, expand_bias, reduce_weight, near_count
        )
        act_far, slope_far, *tied = tie(act_far, slope_far, *sum_near, *pieces_far)
        sum_near, pieces_far = tied[:2], tied[2:]
        swapped = dp_bits[1:2] + dp_bits[:1] + dp_bits[2:]
        reduce_sum = DpSum(n_dp, group, dp_bits)
        expand_sum = DpSum(n_dp, group, swapped)
        output_sum = DpSum(n_dp, group, dp_bits)
        input_sum = DpSum(n_dp, group, dp_bits)
        sum_far = add_up(scatter_near(pieces_far[:near_count], n_mp)).astype(BF16)
        reduce_sum.open([(act_near, grad_near), (act_far, grad_far)])
        sum_far, slope_near, slope_far, act_far = start_all(
            (sum_far, slope_near, slope_far, act_far), [reduce_sum]
        )
        arrived = swap(sum_far, "mp", n_mp, far_bit)
        expand_sum.open([(mlp_near, slope_near), (mlp_far, slope_far)])
        sum_near[0], act_near, act_far, slope_near, slope_far = start_all(
            (sum_near[0], act_near, act_far, slope_near, slope_far), [expand_sum]
        )
        reduce_sum.keep([(act_near, grad_near), (act_far, grad_far)])
        expand_sum.keep([(mlp_near, slope_near), (mlp_far, slope_far)])
        out_far = scatter_near(pieces_far[near_count:], n_mp)
        out_near = scatter_near(pieces_near[near_count:], n_mp)
        held = [reduce_sum.held, expand_sum.held]
        arrived, *held = tie(arrived, *held, *out_far, *out_near)
        reduce_sum.held, expand_sum.held = held[:2]
        out_far, out_near = held[2:4], held[4:]

        normed_grad_two = add_up(sum_near) + arrived.astype(F32)
        grad_out = grad_low.astype(F32)
        residual_grad = grad_out + normalize_back(
            normed_grad_two, normed_two, inverse_two, second_gain
        )
        branch_grad = residual_grad.astype(BF16)
        far_own = swap(branch_grad, "mp", n_mp, far_bit)
        branch_near = gather_near(branch_grad, n_mp)
        head_near = dot_nt(branch_near, output_weight).astype(BF16)
        query_near, key_part, value_part = attend_back(
            near, picks[0], head_near, heads_near, logs_near, [near, far], bars, None, False
        )
        far_own, query_near, normed_grad_two, branch_grad, *out_far = await_all(
            (far_own, query_near, normed_grad_two, branch_grad, *out_far),
            [reduce_sum, expand_sum],
        )
        branch_far = gather_near(far_own, n_mp)
        (branch_far,) = start_all((branch_far,), [reduce_sum, expand_sum])
        branch_pairs = [(heads_near, branch_near), (heads_far, branch_far)]
        output_sum.open(branch_pairs)
        head_far = dot_nt(branch_far, output_weight).astype(BF16)
        (head_far,) = start_all((head_far,), [output_sum])
        query_far, key_grads, value_grads = attend_back(
            far,
            picks[1],
            head_far,
            heads_far,
            logs_far,
            [near, far],
            bars,
            (key_part, value_part),
            True,
        )
        tied = (query_near, branch_far, normed_grad_two, branch_grad, grad_low)
        tied = (query_far, *tied, slope_near, slope_far, *out_far)
        tied = await_all(tied, [reduce_sum, expand_sum])
        query_far, query_near, branch_far, normed_grad_two, branch_grad, grad_low = tied[:6]
        slope_near, slope_far, *out_far = tied[6:]
        qkv_far = jnp.concatenate([query_far, key_grads[1], value_grads[1]], 1)
        sum_far = scatter_near(cut(dot_nt(qkv_far, weight_wide)), n_mp)
        qkv_near = jnp.concatenate([query_near, key_grads[0], value_grads[0]], 1)
        (qkv_near,) = start_all((qkv_near,), [reduce_sum, expand_sum])
        pairs = [(attn_near, qkv_near), (attn_far, qkv_far)]
        input_sum.open(pairs)
        sum_far, qkv_near = start_all((add_up(sum_far).astype(BF16), qkv_near), [input_sum])
        arrived = swap(sum_far, "mp", n_mp, far_bit)
        sum_near = scatter_near(cut(dot_nt(qkv_near, weight_wide)), n_mp)
        input_sum.keep(pairs)
        output_sum.keep([(heads_near, branch_near), (heads_far, branch_far)])
        arrived, input_sum.held, output_sum.held, *sum_near = tie(
            arrived, input_sum.held, output_sum.held, *sum_near
        )
        normed_grad_one = add_up(sum_near) + arrived.astype(F32)
        input_gradient = residual_grad + normalize_back(
            normed_grad_one, normed_one, inverse_one, first_gain
        )
        both = butterfly(
            jnp.stack(
                [
                    jnp.sum(normed_grad_two * normed_two, 0),
                    jnp.sum(normed_grad_two, 0),
                    jnp.sum(branch_grad, 0, dtype=F32),
                    jnp.sum(grad_low, 0, dtype=F32),
                    jnp.sum(normed_grad_one * normed_one, 0),
                    jnp.sum(normed_grad_one, 0),
                ]
            ),
            (("mp", n_mp),),
        )
        hidden = expand_bias.shape[0]
        hidden_sums = jnp.sum(slope_near, 0, dtype=F32) + jnp.sum(slope_far, 0, dtype=F32)
        wide_sums = jnp.sum(qkv_near, 0, dtype=F32) + jnp.sum(qkv_far, 0, dtype=F32)
        small = SmallSum(
            n_dp,
            dp_bits,
            jnp.concatenate(
                [
                    both.reshape(-1),
                    wide_sums[:local_width],
                    wide_sums[2 * local_width :],
                    hidden_sums,
                    jnp.full((PAIR,), jnp.sum(lengths).astype(F32)),
                ]
            ),
        )
        sums = [reduce_sum, expand_sum, input_sum, output_sum]
        token, small.send = await_all((input_gradient, small.send), sums)
        token, *out_far = start_all((token, *out_far), sums[:2])
        token, *out_far = start_all((token, *out_far), sums[2:])
        token, out_far = tie(token, add_up(out_far).astype(BF16))
        out_far = swap(out_far, "mp", n_mp, far_bit)
        quick = [input_sum, output_sum, small]
        slow = [reduce_sum, expand_sum]
        waiting = {"f": quick, "s": slow, "r": slow, "e": [], "R": slow[:1], "E": slow[1:]}
        sending = {"f": quick, "s": slow, "r": slow[:1], "e": slow[1:], "R": [], "E": []}
        flying = list(sums)
        totals = {}
        turns = "fsfsffsf" if len(dp_bits) == 3 else "fs" * 2 * len(dp_bits)
        for n, turn in enumerate(turns):
            if n == 4:
                block_output = (
                    hidden_res + (add_up(out_near) + out_far.astype(F32)) + reduce_bias
                ).astype(BF16)
                token, block_output = tie(token, block_output)
            landing = [s for s in waiting[turn] if s in flying]
            token, out_far = await_all((token, out_far), landing)
            flying = [s for s in flying if s not in landing]
            leaving = [s for s in sending[turn] if s.busy() and s not in flying]
            token, out_far = start_all((token, out_far), leaving)
            flying += leaving
            for s in slow:
                if not (s.busy() or small.busy() or s in totals):
                    factor = lax.rsqrt(small.held[-1])
                    token, totals[s] = tie(token, s.held.astype(F32) * factor)
        if any(s.busy() for s in sums) or flying:
            raise ValueError("unfinished sums")
        input_gradient = token

        total = small.held
        rows = total[: 6 * width].reshape(6, width)
        rest = total[6 * width :]
        factor = lax.rsqrt(rest[2 * local_width + hidden])
        rows = rows * factor
        input_total = input_sum.held.astype(F32) * factor
        return (
            block_output,
            input_gradient,
            rows[4],
            rows[5],
            jnp.stack(
                [input_total[:, t * local_width : (t + 1) * local_width] for t in range(3)]
            ),
            rest[: 2 * local_width].reshape(2, local_width) * factor,
            output_sum.held.astype(F32) * factor,
            rows[2],
            rows[0],
            rows[1],
            totals[expand_sum],
            rest[2 * local_width : 2 * local_width + hidden] * factor,
            totals[reduce_sum],
            rows[3],
        )
    return per_device


def solution(mesh):
    placed = (
        P(("dp", "mp"), None),
        P(("dp", "mp"), None),
        P("dp"),
        P("dp", None),
        P("dp"),
        P(),
        P(),
        P(None, None, "mp"),
        P(None, "mp"),
        P("mp", None),
        P(),
        P(),
        P(),
        P(None, "mp"),
        P("mp"),
        P("mp", None),
        P(),
    )
    return jax.shard_map(
        layer((mesh.shape["dp"], mesh.shape["mp"])),
        mesh=mesh,
        in_specs=placed,
        out_specs=(
            P(("dp", "mp"), None),
            P(("dp", "mp"), None),
            P(),
            P(),
            P(None, None, "mp"),
            P(None, "mp"),
            P("mp", None),
            P(),
            P(),
            P(),
            P(None, "mp"),
            P("mp"),
            P("mp", None),
            P(),
        ),
        check_vma=False,
    )
```

```python
import functools
import jax
import jax.numpy as jnp
from jax import lax
from jax.experimental import pallas as pl
from jax.experimental.pallas import tpu as pltpu
from jax.sharding import PartitionSpec as P

F32 = jnp.float32
BF16 = jnp.bfloat16
PAIR = 128
HD = 64
EXCLUDED = -1e30
LIGHT = pl.CostEstimate(flops=1024, bytes_accessed=1024, transcendentals=0)


def dot_nn(a, b):
    return lax.dot_general(a, b, (((1,), (0,)), ((), ())), preferred_element_type=F32)


def dot_nt(a, b):
    return lax.dot_general(a, b, (((1,), (1,)), ((), ())), preferred_element_type=F32)


def dot_tn(a, b):
    return lax.dot_general(a, b, (((0,), (0,)), ((), ())), preferred_element_type=F32)


def head_lanes(head):
    lane = lax.broadcasted_iota(jnp.int32, (1, PAIR), 1)
    return (lane >= head * HD) & (lane < (head + 1) * HD)


def attend_kernel(halves, q_ref, pick_ref, *refs):
    k_refs, v_refs, bar_refs = (
        refs[:halves],
        refs[halves : 2 * halves],
        refs[2 * halves : 3 * halves],
    )
    out_ref, log_ref = refs[3 * halves :]
    scaled = q_ref[...] * jnp.asarray(HD**-0.5, BF16)
    pick = pick_ref[...]
    keys = [jnp.concatenate([k[...], b[...]], 1) for k, b in zip(k_refs, bar_refs)]
    rows = []
    for head in range(2):
        own = jnp.where(head_lanes(head), scaled, jnp.zeros_like(scaled))
        probe = jnp.concatenate([own, pick], 1)
        scores = [dot_nt(k, probe) for k in keys]
        top = functools.reduce(
            jnp.maximum, [jnp.max(s, 0, keepdims=True) for s in scores]
        )
        powers = [jnp.exp(s - top) for s in scores]
        total = functools.reduce(
            jnp.add, [jnp.sum(p, 0, keepdims=True) for p in powers]
        )
        summed = functools.reduce(
            jnp.add, [dot_tn(v[...], p.astype(BF16)) for v, p in zip(v_refs, powers)]
        )
        rows.append((summed / total)[head * HD : (head + 1) * HD])
        log_ref[0, head : head + 1, :] = top + jnp.log(total)
    out_ref[...] = jnp.concatenate(rows, 0).T.astype(BF16)


def attend_forward(own, pick, halves, bars, tile=512):
    count = own.shape[0]
    width = own.shape[1] // 3
    pairs = width // PAIR
    tile = min(tile, count)
    key_spec = [pl.BlockSpec((h.shape[0], PAIR), lambda p, i: (0, pairs + p)) for h in halves]
    value_spec = [pl.BlockSpec((h.shape[0], PAIR), lambda p, i: (0, 2 * pairs + p)) for h in halves]
    bar_spec = [pl.BlockSpec((b.shape[0], PAIR), lambda p, i: (0, 0)) for b in bars]
    total_keys = sum(h.shape[0] for h in halves)
    return pl.pallas_call(
        functools.partial(attend_kernel, len(halves)),
        grid=(pairs, count // tile),
        in_specs=[
            pl.BlockSpec((tile, PAIR), lambda p, i: (i, p)),
            pl.BlockSpec((tile, PAIR), lambda p, i: (i, 0)),
            *key_spec,
            *value_spec,
            *bar_spec,
        ],
        out_specs=[
            pl.BlockSpec((tile, PAIR), lambda p, i: (i, p)),
            pl.BlockSpec((1, 8, tile), lambda p, i: (p, 0, i)),
        ],
        out_shape=[
            jax.ShapeDtypeStruct((count, width), BF16),
            jax.ShapeDtypeStruct((pairs, 8, count), F32),
        ],
        cost_estimate=LIGHT,
        compiler_params=pltpu.CompilerParams(vmem_limit_bytes=24 * 2**20),
        name="attend_forward",
    )(own, pick, *halves, *halves, *bars)


def attend_back_kernel(halves, first, last, q_ref, pick_ref, grad_ref, out_ref, log_ref, *refs):
    k_refs, v_refs, bar_refs = (
        refs[:halves],
        refs[halves : 2 * halves],
        refs[2 * halves : 3 * halves],
    )
    rest = refs[3 * halves :]
    if not first:
        k_in, v_in = rest[:halves], rest[halves : 2 * halves]
        rest = rest[2 * halves :]
    q_grad_ref = rest[0]
    k_out, v_out = rest[1 : 1 + halves], rest[1 + halves : 1 + 2 * halves]
    if last:
        k_sum, v_sum = (
            rest[1 + 2 * halves : 1 + 3 * halves],
            rest[1 + 3 * halves : 1 + 4 * halves],
        )
    else:
        k_sum, v_sum = k_out, v_out
    step = pl.program_id(1)

    @pl.when(step == 0)
    def _():
        for n in range(halves):
            if first:
                k_sum[n][...] = jnp.zeros_like(k_sum[n])
                v_sum[n][...] = jnp.zeros_like(v_sum[n])
            else:
                k_sum[n][...] = k_in[n][...]
                v_sum[n][...] = v_in[n][...]

    scaled = q_ref[...] * jnp.asarray(HD**-0.5, BF16)
    grad = grad_ref[...]
    pick = pick_ref[...]
    both = (grad.astype(F32) * out_ref[...].astype(F32)).T
    owns = [jnp.where(head_lanes(h), scaled, jnp.zeros_like(scaled)) for h in range(2)]
    grads = [jnp.where(head_lanes(h), grad, jnp.zeros_like(grad)) for h in range(2)]
    probes = [jnp.concatenate([own, pick], 1) for own in owns]
    centers = [jnp.sum(both[h * HD : (h + 1) * HD], 0, keepdims=True) for h in range(2)]
    stacked_q = jnp.concatenate(owns, 0)
    stacked_g = jnp.concatenate(grads, 0)
    q_parts = [0.0, 0.0]
    for n in range(halves):
        keys = k_refs[n][...]
        values = v_refs[n][...]
        wide = jnp.concatenate([keys, bar_refs[n][...]], 1)
        probs = []
        slopes = []
        for h in range(2):
            prob = jnp.exp(dot_nt(wide, probes[h]) - log_ref[0, h : h + 1, :])
            slope = (prob * (dot_nt(values, grads[h]) - centers[h])).astype(BF16)
            probs.append(prob.astype(BF16))
            slopes.append(slope)
            q_parts[h] = q_parts[h] + dot_tn(keys, slope)
        v_sum[n][...] += dot_nn(jnp.concatenate(probs, 1), stacked_g)
        k_sum[n][...] += dot_nn(jnp.concatenate(slopes, 1), stacked_q)
    rows = [q_parts[h][h * HD : (h + 1) * HD] * (HD**-0.5) for h in range(2)]
    q_grad_ref[...] = jnp.concatenate(rows, 0).T.astype(BF16)

    if last:

        @pl.when(step == pl.num_programs(1) - 1)
        def _():
            for n in range(halves):
                k_out[n][...] = k_sum[n][...].astype(BF16)
                v_out[n][...] = v_sum[n][...].astype(BF16)


def attend_back(own, pick, grad, out, logs, halves, bars, carried, last, tile=256):
    count = own.shape[0]
    width = own.shape[1] // 3
    pairs = width // PAIR
    tile = min(tile, count)
    first = carried is None
    key_spec = [pl.BlockSpec((h.shape[0], PAIR), lambda p, i: (0, pairs + p)) for h in halves]
    value_spec = [pl.BlockSpec((h.shape[0], PAIR), lambda p, i: (0, 2 * pairs + p)) for h in halves]
    bar_spec = [pl.BlockSpec((b.shape[0], PAIR), lambda p, i: (0, 0)) for b in bars]
    sum_spec = [pl.BlockSpec((h.shape[0], PAIR), lambda p, i: (0, p)) for h in halves]
    row_spec = pl.BlockSpec((tile, PAIR), lambda p, i: (i, p))
    sum_type = BF16 if last else F32
    sums = [jax.ShapeDtypeStruct((h.shape[0], width), sum_type) for h in halves]
    total_keys = sum(h.shape[0] for h in halves)
    scratch = []
    if last:
        scratch = [pltpu.VMEM((h.shape[0], PAIR), F32) for h in halves] * 2
    extra = [] if first else list(carried[0]) + list(carried[1])
    parts = len(halves)
    result = pl.pallas_call(
        functools.partial(attend_back_kernel, parts, first, last),
        grid=(pairs, count // tile),
        in_specs=[
            row_spec,
            pl.BlockSpec((tile, PAIR), lambda p, i: (i, 0)),
            row_spec,
            row_spec,
            pl.BlockSpec((1, 8, tile), lambda p, i: (p, 0, i)),
            *key_spec,
            *value_spec,
            *bar_spec,
            *([] if first else sum_spec * 2),
        ],
        out_specs=[row_spec, *sum_spec, *sum_spec],
        out_shape=[jax.ShapeDtypeStruct((count, width), BF16), *sums, *sums],
        scratch_shapes=scratch,
        cost_estimate=LIGHT,
        compiler_params=pltpu.CompilerParams(vmem_limit_bytes=24 * 2**20),
        name="attend_back",
    )(own, pick, grad, out, logs, *halves, *halves, *bars, *extra)
    return result[0], result[1 : 1 + parts], result[1 + parts :]


def mlp_kernel(per, x_ref, grad_ref, up_ref, bias_ref, down_ref, act_ref, slope_ref, *piece_refs):
    pre = dot_nn(x_ref[...], up_ref[...]) + bias_ref[...]
    upstream = dot_nt(grad_ref[...], down_ref[...])
    cdf = 0.5 + 0.5 * lax.erf(pre * (0.5**0.5))
    act = (pre * cdf).astype(BF16)
    act_ref[...] = act
    share = dot_nn(act, down_ref[...]).astype(BF16)
    density = jnp.exp(-0.5 * pre * pre) * 0.3989422804014327
    slope = (upstream * (cdf + pre * density)).astype(BF16)
    slope_ref[...] = slope
    back = dot_nt(slope, up_ref[...]).astype(BF16)
    step = pl.program_id(0)
    tile = x_ref.shape[0]
    pieces = len(piece_refs) // 2
    for j in range(pieces):

        @pl.when(step // per == j)
        def _():
            rows = pl.ds(pl.multiple_of((step % per) * tile, tile), tile)
            piece_refs[j][rows, :] = back
            piece_refs[pieces + j][rows, :] = share


def mlp_both(x, grad, up, bias, down, pieces, tile=256):
    count, width = x.shape
    hidden = up.shape[1]
    size = count // pieces
    tile = min(tile, size)
    whole = lambda i: (0, 0)
    return pl.pallas_call(
        functools.partial(mlp_kernel, size // tile),
        grid=(count // tile,),
        in_specs=[
            pl.BlockSpec((tile, width), lambda i: (i, 0)),
            pl.BlockSpec((tile, width), lambda i: (i, 0)),
            pl.BlockSpec((width, hidden), whole, pipeline_mode=pl.Buffered(1)),
            pl.BlockSpec((1, hidden), whole),
            pl.BlockSpec((hidden, width), whole, pipeline_mode=pl.Buffered(1)),
        ],
        out_specs=[
            pl.BlockSpec((tile, hidden), lambda i: (i, 0)),
            pl.BlockSpec((tile, hidden), lambda i: (i, 0)),
            *[pl.BlockSpec((size, width), whole)] * (2 * pieces),
        ],
        out_shape=[
            jax.ShapeDtypeStruct((count, hidden), BF16),
            jax.ShapeDtypeStruct((count, hidden), BF16),
            *[jax.ShapeDtypeStruct((size, width), BF16)] * (2 * pieces),
        ],
        cost_estimate=LIGHT,
        compiler_params=pltpu.CompilerParams(vmem_limit_bytes=24 * 2**20),
        name="mlp_both",
    )(x, grad, up, bias[None], down)


EPSILON = 1e-06


def normalize(values):
    center = values - jnp.mean(values, -1, keepdims=True)
    inverse = lax.rsqrt(jnp.mean(center * center, -1, keepdims=True) + EPSILON)
    return (center * inverse, inverse)


def normalize_back(upstream, normed, inverse, gain):
    scaled = upstream * gain
    return inverse * (
        scaled
        - jnp.mean(scaled, -1, keepdims=True)
        - normed * jnp.mean(scaled * normed, -1, keepdims=True)
    )


def position_rows(own_items, item_lengths, level, first_row, width):
    slot_count = item_lengths.shape[0]
    slot_index = lax.broadcasted_iota(jnp.int32, (1, slot_count), 1)
    start_row = jnp.sum(jnp.where(slot_index < own_items[:, None], item_lengths[None, :], 0), 1)
    row_index = first_row + jnp.arange(own_items.shape[0], dtype=jnp.int32)
    valid_rows = (own_items < slot_count).astype(F32)
    level_ratio = jnp.exp2(level.astype(F32) - 2.0)
    places = (row_index - start_row).astype(F32) * level_ratio
    half_width = width // 2
    frequency = jnp.exp(-jnp.log(10000.0) * jnp.arange(half_width, dtype=F32) / half_width)
    angles = places[:, None] * frequency[None, :]
    return (
        jnp.concatenate([jnp.sin(angles), jnp.cos(angles)], 1) * valid_rows[:, None],
        valid_rows,
    )


def bits_of(size):
    bits = []
    step = 1
    while step < size:
        bits.append(step)
        step *= 2
    return bits


def tie(*arrays):
    return lax.optimization_barrier(arrays)


def swap(array, axis, size, bit):
    return lax.ppermute(array, axis, [(i, i ^ bit) for i in range(size)])


def gather_near(own, count):
    blocks = {0: own}
    for bit in reversed(bits_of(count)[:-1]):
        blocks.update(
            {j | bit: swap(rows, "mp", count, bit) for j, rows in list(blocks.items())}
        )
    return jnp.concatenate([blocks[j] for j in range(count // 2)])


def scatter_near(pieces, count):
    held = dict(enumerate(pieces))
    bits = bits_of(count)[:-1]
    for bit in bits:
        arrived = {
            j ^ bit: swap(held[j].astype(BF16), "mp", count, bit) for j in held if j & bit
        }
        if bit == bits[-1]:
            return held[0], arrived[0]
        held = {j: held[j].astype(F32) + arrived[j].astype(F32) for j in arrived}


def add_up(pair):
    return pair[0].astype(F32) + pair[1].astype(F32)


class DpSum:
    def __init__(self, count, index, order):
        self.count, self.index = count, index
        self.order = order
        self.steps = list(order) + list(reversed(order))
        self.at = 0

    def high(self, bit):
        return (self.index & bit) != 0

    def open(self, pairs):
        total = functools.reduce(jnp.add, [dot_tn(left, right) for left, right in pairs])
        rows, width = total.shape
        halves = total.astype(BF16).reshape(2, rows // 2, width)
        place = self.high(self.order[0]).astype(jnp.int32)
        self.send = lax.dynamic_index_in_dim(halves, 1 - place, 0, False)
        self.held = lax.dynamic_index_in_dim(halves, place, 0, False)

    def keep(self, pairs):
        pass

    def launch(self):
        self.flying = swap(self.send, "dp", self.count, self.steps[self.at])

    def land(self):
        bit = self.steps[self.at]
        if self.at < len(self.order):
            self.held = (self.held.astype(F32) + self.flying.astype(F32)).astype(BF16)
        else:
            self.held = jnp.where(
                self.high(bit),
                jnp.concatenate([self.flying, self.held]),
                jnp.concatenate([self.held, self.flying]),
            )
        self.at += 1
        if self.at < len(self.order):
            rows, width = self.held.shape
            halves = self.held.reshape(2, rows // 2, width)
            place = self.high(self.steps[self.at]).astype(jnp.int32)
            self.send = lax.dynamic_index_in_dim(halves, 1 - place, 0, False)
            self.held = lax.dynamic_index_in_dim(halves, place, 0, False)
        else:
            self.send = self.held

    def busy(self):
        return self.at < len(self.steps)


class SmallSum:
    def __init__(self, count, order, values):
        self.count, self.steps, self.at = count, list(order), 0
        self.send = self.held = values

    def launch(self):
        self.held = self.send
        self.flying = swap(self.send, "dp", self.count, self.steps[self.at])

    def land(self):
        self.send = self.held = self.held + self.flying
        self.at += 1

    def busy(self):
        return self.at < len(self.steps)


def await_all(chain, sums):
    tied = tie(*chain, *[s.flying for s in sums])
    for s, value in zip(sums, tied[len(chain) :]):
        s.flying = value
        s.land()
    return tied[: len(chain)]


def start_all(chain, sums):
    sums = [s for s in sums if s.busy()]
    tied = tie(*chain, *[s.send for s in sums])
    for s, value in zip(sums, tied[len(chain) :]):
        s.send = value
        s.launch()
    return tied[: len(chain)]


def butterfly(values, sizes):
    for axis, size in sizes:
        for bit in bits_of(size):
            values = values + swap(values, axis, size, bit)
    return values


def layer(sizes):
    n_dp, n_mp = sizes
    far_bit = n_mp // 2
    dp_bits = bits_of(n_dp)

    def per_device(
        tokens,
        cotangent,
        segments,
        lengths,
        scale_levels,
        first_gain,
        first_shift,
        input_weight,
        input_bias,
        output_weight,
        output_bias,
        second_gain,
        second_shift,
        expand_weight,
        expand_bias,
        reduce_weight,
        reduce_bias,
    ):
        me = lax.axis_index("mp")
        group = lax.axis_index("dp")
        own_count, width = tokens.shape
        local_width = input_weight.shape[2]
        half_count = own_count * n_mp // 2
        item_blocks = [
            lax.dynamic_slice_in_dim(segments, (me ^ j) * own_count, own_count)
            for j in range(n_mp)
        ]
        positions, valid_rows = position_rows(
            item_blocks[0], lengths[0], scale_levels[0], me * own_count, width
        )
        residual = tokens.astype(F32) + positions
        normed_one, inverse_one = normalize(residual)
        attn_input = (normed_one * first_gain + first_shift).astype(BF16)
        grad_low = (cotangent.astype(F32) * valid_rows[:, None]).astype(BF16)

        far_own = swap(attn_input, "mp", n_mp, far_bit)
        attn_near = gather_near(attn_input, n_mp)
        lanes = lax.broadcasted_iota(jnp.int32, (1, PAIR), 1)
        half_items = [
            jnp.concatenate(item_blocks[: n_mp // 2]),
            jnp.concatenate(item_blocks[n_mp // 2 :]),
        ]
        picks = [(items[:, None] == lanes).astype(BF16) for items in half_items]
        bars = [
            jnp.where(items[:, None] == lanes, 0.0, EXCLUDED).astype(BF16) for items in half_items
        ]
        bias_wide = jnp.concatenate([input_bias[0], jnp.zeros_like(input_bias[0]), input_bias[1]])
        weight_wide = jnp.concatenate([input_weight[0], input_weight[1], input_weight[2]], 1)

        def project(rows):
            return (dot_nn(rows, weight_wide) + bias_wide).astype(BF16)

        near = project(attn_near)
        far_own, near, grad_low = tie(far_own, near, grad_low)
        attn_far = gather_near(far_own, n_mp)
        grad_far = swap(grad_low, "mp", n_mp, far_bit)
        far = project(attn_far)

        heads_far, logs_far = attend_forward(far, picks[1], [near, far], bars)
        near_count = n_mp // 2

        def cut(rows):
            rows = rows.astype(BF16)
            return [rows[j * own_count : (j + 1) * own_count] for j in range(near_count)]

        sum_far = add_up(scatter_near(cut(dot_nn(heads_far, output_weight)), n_mp)).astype(BF16)
        sum_far, near = tie(sum_far, near)
        arrived = swap(sum_far, "mp", n_mp, far_bit)
        heads_near, logs_near = attend_forward(near, picks[0], [near, far], bars)
        sum_near = scatter_near(cut(dot_nn(heads_near, output_weight)), n_mp)
        grad_near = gather_near(grad_low, n_mp)
        grad_far = gather_near(grad_far, n_mp)
        arrived, grad_near, grad_far = tie(arrived, grad_near, grad_far)
        hidden_res = residual + (add_up(sum_near) + arrived.astype(F32)) + output_bias
        normed_two, inverse_two = normalize(hidden_res)
        mlp_input = (normed_two * second_gain + second_shift).astype(BF16)

        far_own = swap(mlp_input, "mp", n_mp, far_bit)
        mlp_near = gather_near(mlp_input, n_mp)
        act_near, slope_near, *pieces_near = mlp_both(
            mlp_near, grad_near, expand_weight, expand_bias, reduce_weight, near_count
        )
        far_own, act_near, slope_near, *pieces_near = tie(
            far_own, act_near, slope_near, *pieces_near
        )
        mlp_far = gather_near(far_own, n_mp)
        sum_near = scatter_near(pieces_near[:near_count], n_mp)
        act_far, slope_far, *pieces_far = mlp_both(
            mlp_far, grad_far, expand_weight, expand_bias, reduce_weight, near_count
        )
        act_far, slope_far, *tied = tie(act_far, slope_far, *sum_near, *pieces_far)
        sum_near, pieces_far = tied[:2], tied[2:]
        swapped = dp_bits[1:2] + dp_bits[:1] + dp_bits[2:]
        reduce_sum = DpSum(n_dp, group, dp_bits)
        expand_sum = DpSum(n_dp, group, swapped)
        output_sum = DpSum(n_dp, group, dp_bits)
        input_sum = DpSum(n_dp, group, dp_bits)
        sum_far = add_up(scatter_near(pieces_far[:near_count], n_mp)).astype(BF16)
        reduce_sum.open([(act_near, grad_near), (act_far, grad_far)])
        sum_far, slope_near, slope_far, act_far = start_all(
            (sum_far, slope_near, slope_far, act_far), [reduce_sum]
        )
        arrived = swap(sum_far, "mp", n_mp, far_bit)
        expand_sum.open([(mlp_near, slope_near), (mlp_far, slope_far)])
        sum_near[0], act_near, act_far, slope_near, slope_far = start_all(
            (sum_near[0], act_near, act_far, slope_near, slope_far), [expand_sum]
        )
        reduce_sum.keep([(act_near, grad_near), (act_far, grad_far)])
        expand_sum.keep([(mlp_near, slope_near), (mlp_far, slope_far)])
        out_far = scatter_near(pieces_far[near_count:], n_mp)
        out_near = scatter_near(pieces_near[near_count:], n_mp)
        held = [reduce_sum.held, expand_sum.held]
        arrived, *held = tie(arrived, *held, *out_far, *out_near)
        reduce_sum.held, expand_sum.held = held[:2]
        out_far, out_near = held[2:4], held[4:]

        normed_grad_two = add_up(sum_near) + arrived.astype(F32)
        grad_out = grad_low.astype(F32)
        residual_grad = grad_out + normalize_back(
            normed_grad_two, normed_two, inverse_two, second_gain
        )
        branch_grad = residual_grad.astype(BF16)
        far_own = swap(branch_grad, "mp", n_mp, far_bit)
        branch_near = gather_near(branch_grad, n_mp)
        head_near = dot_nt(branch_near, output_weight).astype(BF16)
        query_near, key_part, value_part = attend_back(
            near, picks[0], head_near, heads_near, logs_near, [near, far], bars, None, False
        )
        far_own, query_near, normed_grad_two, branch_grad, *out_far = await_all(
            (far_own, query_near, normed_grad_two, branch_grad, *out_far),
            [reduce_sum, expand_sum],
        )
        branch_far = gather_near(far_own, n_mp)
        (branch_far,) = start_all((branch_far,), [reduce_sum, expand_sum])
        branch_pairs = [(heads_near, branch_near), (heads_far, branch_far)]
        output_sum.open(branch_pairs)
        head_far = dot_nt(branch_far, output_weight).astype(BF16)
        (head_far,) = start_all((head_far,), [output_sum])
        query_far, key_grads, value_grads = attend_back(
            far,
            picks[1],
            head_far,
            heads_far,
            logs_far,
            [near, far],
            bars,
            (key_part, value_part),
            True,
        )
        tied = (query_near, branch_far, normed_grad_two, branch_grad, grad_low)
        tied = (query_far, *tied, slope_near, slope_far, *out_far)
        tied = await_all(tied, [reduce_sum, expand_sum])
        query_far, query_near, branch_far, normed_grad_two, branch_grad, grad_low = tied[:6]
        slope_near, slope_far, *out_far = tied[6:]
        qkv_far = jnp.concatenate([query_far, key_grads[1], value_grads[1]], 1)
        sum_far = scatter_near(cut(dot_nt(qkv_far, weight_wide)), n_mp)
        qkv_near = jnp.concatenate([query_near, key_grads[0], value_grads[0]], 1)
        (qkv_near,) = start_all((qkv_near,), [reduce_sum, expand_sum])
        pairs = [(attn_near, qkv_near), (attn_far, qkv_far)]
        input_sum.open(pairs)
        sum_far, qkv_near = start_all((add_up(sum_far).astype(BF16), qkv_near), [input_sum])
        arrived = swap(sum_far, "mp", n_mp, far_bit)
        sum_near = scatter_near(cut(dot_nt(qkv_near, weight_wide)), n_mp)
        input_sum.keep(pairs)
        output_sum.keep([(heads_near, branch_near), (heads_far, branch_far)])
        arrived, input_sum.held, output_sum.held, *sum_near = tie(
            arrived, input_sum.held, output_sum.held, *sum_near
        )
        normed_grad_one = add_up(sum_near) + arrived.astype(F32)
        input_gradient = residual_grad + normalize_back(
            normed_grad_one, normed_one, inverse_one, first_gain
        )
        both = butterfly(
            jnp.stack(
                [
                    jnp.sum(normed_grad_two * normed_two, 0),
                    jnp.sum(normed_grad_two, 0),
                    jnp.sum(branch_grad, 0, dtype=F32),
                    jnp.sum(grad_low, 0, dtype=F32),
                    jnp.sum(normed_grad_one * normed_one, 0),
                    jnp.sum(normed_grad_one, 0),
                ]
            ),
            (("mp", n_mp),),
        )
        hidden = expand_bias.shape[0]
        hidden_sums = jnp.sum(slope_near, 0, dtype=F32) + jnp.sum(slope_far, 0, dtype=F32)
        wide_sums = jnp.sum(qkv_near, 0, dtype=F32) + jnp.sum(qkv_far, 0, dtype=F32)
        small = SmallSum(
            n_dp,
            dp_bits,
            jnp.concatenate(
                [
                    both.reshape(-1),
                    wide_sums[:local_width],
                    wide_sums[2 * local_width :],
                    hidden_sums,
                    jnp.full((PAIR,), jnp.sum(lengths).astype(F32)),
                ]
            ),
        )
        sums = [reduce_sum, expand_sum, input_sum, output_sum]
        (token,) = await_all((input_gradient,), sums)
        token, *out_far = start_all((token, *out_far), sums[:2])
        token, *out_far = start_all((token, *out_far), sums[2:])
        token, out_far, small.send = tie(token, add_up(out_far).astype(BF16), small.send)
        out_far = swap(out_far, "mp", n_mp, far_bit)
        quick = [input_sum, output_sum, small]
        slow = [reduce_sum, expand_sum]
        waiting = {"f": quick, "s": slow, "r": slow, "e": [], "R": slow[:1], "E": slow[1:]}
        sending = {"f": quick, "s": slow, "r": slow[:1], "e": slow[1:], "R": [], "E": []}
        flying = list(sums)
        totals = {}
        turns = "fsfsffsf" if len(dp_bits) == 3 else "fs" * 2 * len(dp_bits)
        for n, turn in enumerate(turns):
            if n == 4:
                block_output = (
                    hidden_res + (add_up(out_near) + out_far.astype(F32)) + reduce_bias
                ).astype(BF16)
                token, block_output = tie(token, block_output)
            landing = [s for s in waiting[turn] if s in flying]
            token, out_far = await_all((token, out_far), landing)
            flying = [s for s in flying if s not in landing]
            leaving = [s for s in sending[turn] if s.busy() and s not in flying]
            token, out_far = start_all((token, out_far), leaving)
            flying += leaving
            for s in slow:
                if not (s.busy() or small.busy() or s in totals):
                    factor = lax.rsqrt(small.held[-1])
                    token, totals[s] = tie(token, s.held.astype(F32) * factor)
        if any(s.busy() for s in sums) or flying:
            raise ValueError("unfinished sums")
        input_gradient = token

        total = small.held
        rows = total[: 6 * width].reshape(6, width)
        rest = total[6 * width :]
        factor = lax.rsqrt(rest[2 * local_width + hidden])
        rows = rows * factor
        input_total = input_sum.held.astype(F32) * factor
        return (
            block_output,
            input_gradient,
            rows[4],
            rows[5],
            jnp.stack(
                [input_total[:, t * local_width : (t + 1) * local_width] for t in range(3)]
            ),
            rest[: 2 * local_width].reshape(2, local_width) * factor,
            output_sum.held.astype(F32) * factor,
            rows[2],
            rows[0],
            rows[1],
            totals[expand_sum],
            rest[2 * local_width : 2 * local_width + hidden] * factor,
            totals[reduce_sum],
            rows[3],
        )
    return per_device


def solution(mesh):
    placed = (
        P(("dp", "mp"), None),
        P(("dp", "mp"), None),
        P("dp"),
        P("dp", None),
        P("dp"),
        P(),
        P(),
        P(None, None, "mp"),
        P(None, "mp"),
        P("mp", None),
        P(),
        P(),
        P(),
        P(None, "mp"),
        P("mp"),
        P("mp", None),
        P(),
    )
    return jax.shard_map(
        layer((mesh.shape["dp"], mesh.shape["mp"])),
        mesh=mesh,
        in_specs=placed,
        out_specs=(
            P(("dp", "mp"), None),
            P(("dp", "mp"), None),
            P(),
            P(),
            P(None, None, "mp"),
            P(None, "mp"),
            P("mp", None),
            P(),
            P(),
            P(),
            P(None, "mp"),
            P("mp"),
            P("mp", None),
            P(),
        ),
        check_vma=False,
    )
```
